256 devices in a mesh: grid: 64 (over z, y, core), sub: 4 (over x).
Axes of the slice: x: 4, y: 4, z: 8, core: 2. Of those that a mesh axis runs over, the one named last changes fastest.
Arguments:
- field: float32 [5, 2048, 32, 128], P(None, ('grid', 'sub')), may hold values from -6 to 6
- node_jitter: float32 [3, 2048, 32, 128], P(None, ('grid', 'sub')), may hold values from -0.15 to 0.15
- time_ratio: float32 [2048, 32, 128], P(('grid', 'sub')), may hold values from 0.2 to 5
- donor_cell: int32 [256, 64, 2, 128], P(('grid', 'sub')), may hold values from 0 to 32638, as said below
- receptor_offset: float32 [256, 64, 2, 3, 128], P(('grid', 'sub')), may hold values from 0.1 to 0.9
- receptor_node: int32 [256, 64, 2, 128], P(('grid', 'sub')), may hold values from 4096 to 28671, as said below
- point_count: int32 [256, 64], P(('grid', 'sub')), may hold values from 1 to 256, as said below
Outputs:
- relaxed: float32 [5, 2048, 32, 128], P(None, ('grid', 'sub'))
The draws below stay inside these ranges and needn't reach their ends.
Inputs may be any that keep to these rules, and one draw needn't show every extreme that they name: `donor_cell`: a cell i * 32 * 128 + j * 128 + k with i < 8, j < 31, k < 127. `receptor_node`: distinct over all slots of one source block, on local planes 1 to 6. `point_count`: from every block of grid g, owner (g + 1) mod 64 receives exactly 256 points, owner (g + 2) mod 64 receives one point, and every other owner at most 128.
All inputs are finite; a program needn't handle non-finite values.
Results may differ from the reference program's by a relative error of at most 0.0003.
Values sent between devices are 32-bit elements; how exact they have to be, the bound alone decides.
A program may use at most 128 MiB of HBM per device.

```python
import math
import jax
import jax.numpy as jnp
from jax import lax

NV = 5
PTS = 128
CX = 8
CY = 32
CZ = 128
SLOTS = 2
OWNERS = 64
SUBS = 4
SOURCES = 256
PLANES = 2048


def draw_donor_cell(key, part):
    key_plane, key_row, key_col, key_low, key_high = jax.random.split(key, 5)
    shape_all = (SOURCES, OWNERS, SLOTS, PTS)
    plane_id = jax.random.randint(key_plane, shape_all, 0, CX)
    row_id = jax.random.randint(key_row, shape_all, 0, CY - 1)
    col_id = jax.random.randint(key_col, shape_all, 0, CZ - 1)
    cells = (plane_id * CY * CZ + row_id * CZ + col_id).astype(jnp.int32).reshape(-1)
    total = SOURCES * OWNERS * SLOTS * PTS
    half = total // 2
    low_place = jax.random.randint(key_low, (), 0, half)
    high_place = jax.random.randint(key_high, (), half, total)
    top_cell = (CX - 1) * CY * CZ + (CY - 2) * CZ + CZ - 2
    cells = cells.at[low_place].set(0)
    cells = cells.at[high_place].set(top_cell)
    return cells.reshape(shape_all).astype(jnp.int32)


def draw_receptor_node(key, part):
    source_keys = jax.random.split(key, SOURCES)
    interior = (CX - 2) * CY * CZ
    needed = OWNERS * SLOTS * PTS

    def one_source(source_key):
        return jax.random.permutation(source_key, interior)[:needed]
    chosen = jax.vmap(one_source)(source_keys) + CY * CZ
    return chosen.reshape(SOURCES, OWNERS, SLOTS, PTS).astype(jnp.int32)


def draw_point_count(key, part):
    key_level, key_base = jax.random.split(key, 2)
    level = jax.random.randint(key_level, (OWNERS,), 1, 5)
    base = jax.random.randint(key_base, (SOURCES, OWNERS), PTS // 8, PTS // 4 + 1)
    counts = jnp.clip(base * level[None, :], 1, PTS)
    grid_of = jnp.arange(SOURCES, dtype=jnp.int32)[:, None] // SUBS
    owner_ids = jnp.arange(OWNERS, dtype=jnp.int32)[None, :]
    heavy = owner_ids == (grid_of + 1) % OWNERS
    single = owner_ids == (grid_of + 2) % OWNERS
    counts = jnp.where(single, 1, counts)
    counts = jnp.where(heavy, SLOTS * PTS, counts)
    return counts.astype(jnp.int32)


def block_levels(rng, dims, pieces, smallest, top_value):
    level = 1.0
    for dim, parts in pieces:
        heights = jax.random.uniform(jax.random.fold_in(jax.random.fold_in(rng, 6), dim), (parts,), jnp.float32, smallest / len(pieces), top_value / len(pieces))
        level = level * jnp.repeat(jnp.exp(heights), dims[dim] // parts).reshape((-1,) + (1,) * (len(dims) - 1 - dim))
    return level


def centred(rng, dims, scale, bound, cuts=(), kind=jnp.bfloat16):
    values = jax.random.normal(rng, dims, jnp.float32) * scale
    if len(cuts) > 0:
        values = block_levels(rng, dims, cuts, -0.22, 0.18) * values
    return jnp.clip(values, min=-bound, max=bound).astype(kind)


def setup_inputs(seed: int = 0) -> dict:
    key_of = jax.random.split(jax.random.key(seed), 8)
    field = centred(key_of[0], (NV, PLANES, CY, CZ), 1.0, 6.0, ((1, 256),), jnp.float32)
    node_jitter = jnp.clip(jax.random.uniform(key_of[1], (3, PLANES, CY, CZ), jnp.float32, -0.15, 0.15) * block_levels(key_of[1], (3, PLANES, CY, CZ), ((1, 256),), -0.4, 0.0), -0.15, 0.15)
    time_ratio = jnp.clip(jnp.exp(math.log(5.0) - 3.218876 * jax.random.uniform(key_of[2], (PLANES, CY, CZ), jnp.float32) ** block_levels(key_of[2], (PLANES, CY, CZ), ((0, 256),), -0.2, 0.2)), 0.2, 5.0)
    donor_cell = draw_donor_cell(jax.random.fold_in(key_of[7], 71), 0)
    receptor_offset = jnp.clip(0.1 + 0.79999997 * jax.random.uniform(key_of[4], (SOURCES, OWNERS, SLOTS, 3, PTS), jnp.float32) ** block_levels(key_of[4], (SOURCES, OWNERS, SLOTS, 3, PTS), ((0, 256),), -0.2, 0.2), 0.1, 0.9)
    receptor_node = draw_receptor_node(jax.random.fold_in(key_of[7], 71), 0)
    point_count = draw_point_count(jax.random.fold_in(key_of[7], 71), 0)
    return {"field": field, "node_jitter": node_jitter, "time_ratio": time_ratio, "donor_cell": donor_cell, "receptor_offset": receptor_offset, "receptor_node": receptor_node, "point_count": point_count}


def corner_bits(corner):
    return (corner >> 2) & 1, (corner >> 1) & 1, corner & 1


def shape_values(param):
    result = []
    for corner in range(8):
        offset_bits = corner_bits(corner)
        factors = [param[axis_id] if offset_bits[axis_id] else 1.0 - param[axis_id] for axis_id in range(3)]
        derivs = [1.0 if offset_bits[axis_id] else -1.0 for axis_id in range(3)]
        weight = factors[0] * factors[1] * factors[2]
        slopes = [derivs[0] * factors[1] * factors[2], factors[0] * derivs[1] * factors[2], factors[0] * factors[1] * derivs[2]]
        result.append((weight, slopes))
    return result


def determinant(matrix):
    return (matrix[0][0] * (matrix[1][1] * matrix[2][2] - matrix[1][2] * matrix[2][1])
            - matrix[0][1] * (matrix[1][0] * matrix[2][2] - matrix[1][2] * matrix[2][0])
            + matrix[0][2] * (matrix[1][0] * matrix[2][1] - matrix[1][1] * matrix[2][0]))


def solve_point(corners, offsets):
    target = [offsets[..., component, :] for component in range(3)]
    places = [[corners[corner, component] + float(corner_bits(corner)[component]) for component in range(3)] for corner in range(8)]
    param = [jnp.full(target[0].shape, 0.5, target[0].dtype) for component in range(3)]
    for newton_step in range(4):
        shapes = shape_values(param)
        misfit = []
        jacobian = []
        for component in range(3):
            position = shapes[0][0] * places[0][component]
            for corner in range(1, 8):
                position = position + shapes[corner][0] * places[corner][component]
            misfit.append(position - target[component])
            jac_row = []
            for direction in range(3):
                slope_sum = shapes[0][1][direction] * places[0][component]
                for corner in range(1, 8):
                    slope_sum = slope_sum + shapes[corner][1][direction] * places[corner][component]
                jac_row.append(slope_sum)
            jacobian.append(jac_row)
        jac_det = determinant(jacobian)
        updates = []
        for direction in range(3):
            replaced = [[misfit[component] if column == direction else jacobian[component][column] for column in range(3)] for component in range(3)]
            updates.append(determinant(replaced) / jac_det)
        param = [param[direction] - updates[direction] for direction in range(3)]
    shapes = shape_values(param)
    values = []
    for variable in range(corners.shape[1] - 3):
        blended = shapes[0][0] * corners[0, 3 + variable]
        for corner in range(1, 8):
            blended = blended + shapes[corner][0] * corners[corner, 3 + variable]
        values.append(blended)
    return jnp.stack(values, axis=-2)


def fill_fringe(own, values, nodes, counts):
    width = own.shape[0]
    interp = jnp.moveaxis(values, 2, 0).reshape(width, -1)
    slot_count, point_total = nodes.shape[1], nodes.shape[2]
    position = jnp.arange(slot_count, dtype=jnp.int32)[:, None] * point_total + jnp.arange(point_total, dtype=jnp.int32)[None, :]
    live = (position[None] < counts[:, None, None]).reshape(-1)
    flat_nodes = nodes.reshape(-1)
    current = own[:, flat_nodes]
    own = own.at[:, flat_nodes].set(jnp.where(live[None], interp, current))
    flags = jnp.zeros((own.shape[1],), own.dtype).at[flat_nodes].set(live.astype(own.dtype))
    return own, flags


def neighbour_sum(above, below, filled):
    lead = [(0, 0)] * (filled.ndim - 2)
    padded_y = jnp.pad(filled, lead + [(1, 1), (0, 0)])
    padded_z = jnp.pad(filled, lead + [(0, 0), (1, 1)])
    return (above + below + padded_y[..., 2:, :] + padded_y[..., :-2, :]
            + padded_z[..., 2:] + padded_z[..., :-2])


def relax(filled, above, below, ratio, flags):
    smooth = (filled + ratio * neighbour_sum(above, below, filled)) / (1.0 + 6.0 * ratio)
    return jnp.where(flags > 0.5, filled, smooth)


def reference(field, node_jitter, time_ratio, donor_cell, receptor_offset, receptor_node, point_count):
    stacked = jnp.concatenate([node_jitter, field], 0)
    blocks = stacked.reshape(8, OWNERS, SUBS, CX, CY, CZ)
    following = jnp.roll(blocks[:, :, :, :1], -1, axis=2)
    extended = jnp.concatenate([blocks, following], axis=3)
    ext_flat = extended.reshape(8, OWNERS, SUBS, (CX + 1) * CY * CZ)
    own_fields = field.reshape(NV, SOURCES, CX * CY * CZ)
    owner_ids = jnp.arange(OWNERS, dtype=jnp.int32)[:, None, None]

    def one_block(source):
        sub_id = source % SUBS
        donor_data = jnp.take(ext_flat, sub_id, axis=2)
        cells = donor_cell[source]
        picks = []
        for corner in range(8):
            offset_bits = corner_bits(corner)
            shift_amount = offset_bits[0] * CY * CZ + offset_bits[1] * CZ + offset_bits[2]
            picks.append(donor_data[:, owner_ids, cells + shift_amount])
        corners = jnp.stack(picks, 0)
        values = solve_point(corners, receptor_offset[source])
        own = jnp.take(own_fields, source, axis=1)
        return fill_fringe(own, values, receptor_node[source], point_count[source])

    filled, flags = lax.map(one_block, jnp.arange(SOURCES, dtype=jnp.int32))
    filled = jnp.moveaxis(filled, 0, 1).reshape(NV, OWNERS, SUBS * CX, CY, CZ)
    flags = flags.reshape(OWNERS, SUBS * CX, CY, CZ)
    ratio = time_ratio.reshape(OWNERS, SUBS * CX, CY, CZ)
    above = jnp.roll(filled, -1, axis=2)
    below = jnp.roll(filled, 1, axis=2)
    relaxed = relax(filled, above, below, ratio, flags)
    return relaxed.reshape(NV, PLANES, CY, CZ)
```

```python
import jax
import jax.numpy as jnp
from jax import lax
from jax.experimental import pallas as pl
from jax.experimental.pallas import tpu as pltpu
from jax.sharding import PartitionSpec as P

LANES = 128
TILE = 8
ROWS = 32
CELL_PLANES = 8
PLANE = ROWS * LANES
NV = 5
UNROLL = 16
HALF_CELLS = CELL_PLANES // 2 * PLANE
FILL_ROWS = (CELL_PLANES - 2) * PLANE // 16


def lerp(low, high, weight):
    return low + weight * (high - low)


def solve_group(places, target):
    size = target[0].shape
    param = [jnp.full(size, 0.5, jnp.float32) for _ in range(3)]
    rise = [
        [[places[m][a][b][1] - places[m][a][b][0] for b in range(2)] for a in range(2)]
        for m in range(3)
    ]
    for _ in range(4):
        u, v, w = param
        misfit, jac = [], []
        for m in range(3):
            edge = [[places[m][a][b][0] + w * rise[m][a][b] for b in range(2)] for a in range(2)]
            across = [edge[a][1] - edge[a][0] for a in range(2)]
            face = [edge[a][0] + v * across[a] for a in range(2)]
            slope0 = face[1] - face[0]
            misfit.append(face[0] + u * slope0 - target[m])
            slope1 = lerp(across[0], across[1], u)
            slope2 = lerp(
                lerp(rise[m][0][0], rise[m][0][1], v), lerp(rise[m][1][0], rise[m][1][1], v), u
            )
            jac.append((slope0, slope1, slope2))
        x, y, z = ([jac[m][d] for m in range(3)] for d in range(3))

        def cross(p, q):
            return [
                p[1] * q[2] - p[2] * q[1],
                p[2] * q[0] - p[0] * q[2],
                p[0] * q[1] - p[1] * q[0],
            ]

        def dot(p, q):
            return p[0] * q[0] + p[1] * q[1] + p[2] * q[2]

        yz, zx, xy = cross(y, z), cross(z, x), cross(x, y)
        inverse = 1.0 / dot(x, yz)
        param = [
            u - dot(misfit, yz) * inverse,
            v - dot(misfit, zx) * inverse,
            w - dot(misfit, xy) * inverse,
        ]
    return param


def donor_kernel(
    cells, counts, cell_rows, field, jitter, ahead, offsets, extra_offsets, out,
    tiles, shifted, table, picked, corners,
):
    blocks = counts.shape[0]

    def fill(tile, carry):
        base = pl.multiple_of(tile * TILE, TILE)
        for c in range(8):
            data = field[c, pl.ds(base, TILE), :] if c < NV else jitter[c - NV, pl.ds(base, TILE), :]
            tiles[pl.ds(base * TILE + c, TILE, stride=TILE), :] = data
            shifted[pl.ds(base * TILE + c, TILE, stride=TILE), :] = pltpu.roll(data, LANES - 1, 1)
        return carry

    lax.fori_loop(0, CELL_PLANES * ROWS // TILE, fill, 0)
    for tile in range(ROWS // TILE):
        for c in range(8):
            start = (CELL_PLANES * ROWS + tile * TILE) * TILE + c
            data = ahead[c, pl.ds(tile * TILE, TILE), :]
            tiles[pl.ds(start, TILE, stride=TILE), :] = data
            shifted[pl.ds(start, TILE, stride=TILE), :] = pltpu.roll(data, LANES - 1, 1)

    def build(row, carry):
        parts = []
        for half in range(2):
            for a in (0, 1, ROWS, ROWS + 1):
                start = pl.multiple_of((row + half * (CELL_PLANES // 2) * ROWS + a) * TILE, TILE)
                parts.append(tiles[pl.ds(start, TILE), :])
                parts.append(shifted[pl.ds(start, TILE), :])
        table[pl.ds(pl.multiple_of(row * LANES, LANES), LANES), :] = jnp.concatenate(parts, 0).T
        return carry

    def build_some(q, carry):
        for step in range(4):
            build(q * 4 + step, 0)
        return carry

    lax.fori_loop(0, HALF_CELLS // LANES // 4, build_some, 0)

    def gather_block(b, carry):
        def chunk(q, carry):
            first = pl.multiple_of(b * LANES + q * UNROLL, UNROLL)
            for step in range(UNROLL):
                row = cells[first + step] & (HALF_CELLS - 1)
                picked[pl.ds(first + step, 1), :] = table[pl.ds(row, 1), :]
            return carry

        return lax.fori_loop(0, (counts[b] + UNROLL - 1) // UNROLL, chunk, carry)

    lax.fori_loop(0, blocks, gather_block, 0)

    def turn(b):
        values = picked[pl.ds(pl.multiple_of(b * LANES, LANES), LANES), :].T
        far = cell_rows[pl.ds(b, 1), :] >= HALF_CELLS
        start = pl.multiple_of(b * TILE, TILE)
        for q in range(8):
            corners[q, pl.ds(start, TILE), :] = jnp.where(
                far, values[64 + 8 * q : 72 + 8 * q], values[8 * q : 8 * q + 8]
            )

    def turn_some(g, carry):
        for step in range(4):
            turn(g * 4 + step)
        return carry

    lax.fori_loop(0, (blocks - 1) // 4, turn_some, 0)
    turn(blocks - 1)

    def solve(first, target):
        base = first * TILE
        places = [
            [
                [
                    [
                        corners[4 * a + 2 * b + d, pl.ds(base + NV + m, TILE, stride=TILE), :]
                        + float((a, b, d)[m])
                        for d in range(2)
                    ]
                    for b in range(2)
                ]
                for a in range(2)
            ]
            for m in range(3)
        ]
        u, v, w = solve_group(places, target)
        for c in range(NV):
            node = [
                corners[q, pl.ds(base + c, TILE, stride=TILE), :] for q in range(8)
            ]
            edge = [lerp(node[2 * e], node[2 * e + 1], w) for e in range(4)]
            value = lerp(lerp(edge[0], edge[1], v), lerp(edge[2], edge[3], v), u)
            out[pl.ds(base + c, TILE, stride=TILE), :] = value

    def solve_step(g, carry):
        first = pl.multiple_of(g * TILE, TILE)
        solve(first, [offsets[m, pl.ds(first, TILE), :] for m in range(3)])
        return carry

    lax.fori_loop(0, (blocks - 1) // TILE, solve_step, 0)
    solve(
        blocks - 1,
        [jnp.broadcast_to(extra_offsets[m : m + 1, :], (TILE, LANES)) for m in range(3)],
    )


def donor_values(cells, counts, field, jitter, ahead, offsets, extra_offsets):
    blocks = counts.shape[0]
    padded = blocks - 1 + TILE
    node_rows = (CELL_PLANES + 1) * ROWS
    vmem = pl.BlockSpec(memory_space=pltpu.VMEM)
    smem = pl.BlockSpec(memory_space=pltpu.SMEM)
    return pl.pallas_call(
        donor_kernel,
        out_shape=jax.ShapeDtypeStruct((padded * TILE, LANES), jnp.float32),
        in_specs=[smem, smem] + [vmem] * 6,
        out_specs=vmem,
        scratch_shapes=[
            pltpu.VMEM((node_rows * TILE + 2 * TILE, LANES), jnp.float32),
            pltpu.VMEM((node_rows * TILE + 2 * TILE, LANES), jnp.float32),
            pltpu.VMEM((HALF_CELLS, LANES), jnp.float32),
            pltpu.VMEM((blocks * LANES, LANES), jnp.float32),
            pltpu.VMEM((8, padded * TILE, LANES), jnp.float32),
        ],
        compiler_params=pltpu.CompilerParams(vmem_limit_bytes=48 << 20),
        name="donor",
    )(cells.reshape(-1), counts, cells, field, jitter, ahead, offsets, extra_offsets)


def fill_kernel(
    marks, counts, values, extra_values, field, behind, ahead, ratio, out,
    blocks_in, turned, rows, filled, fringes,
):
    owners = counts.shape[0] - 1
    size = CELL_PLANES * ROWS
    group = lax.broadcasted_iota(jnp.int32, (1, LANES), 1) >> 3
    lane = lax.broadcasted_iota(jnp.int32, (TILE, LANES), 1)
    level = lax.broadcasted_iota(jnp.int32, (TILE, LANES), 0)

    def pad(o, carry):
        start = pl.multiple_of(o * TILE, TILE)
        blocks_in[pl.ds(start, TILE), :] = jnp.ones((TILE, LANES), jnp.float32)
        blocks_in[pl.ds(start, NV), :] = values[o]
        return carry

    lax.fori_loop(0, owners, pad, 0)
    blocks_in[pl.ds(owners * TILE, TILE), :] = jnp.where(level < NV, extra_values[...], 1.0)

    def clear(q, carry):
        rows[pl.ds(pl.multiple_of(q * LANES, LANES), LANES), :] = jnp.zeros(
            (LANES, LANES), jnp.float32
        )
        return carry

    lax.fori_loop(0, FILL_ROWS // LANES, clear, 0)

    def spread(o):
        block = blocks_in[pl.ds(pl.multiple_of(o * TILE, TILE), TILE), :]
        start = pl.multiple_of(o * LANES, LANES)
        turned[pl.ds(start, LANES), :] = jnp.concatenate([block] * 16, 0).T

    def spread_some(g, carry):
        for step in range(4):
            spread(g * 4 + step)
        return carry

    lax.fori_loop(0, owners // 4, spread_some, 0)
    spread(owners)

    def scatter(o, carry):
        def chunk(q, carry):
            first = pl.multiple_of(o * LANES + q * UNROLL, UNROLL)
            for step in range(UNROLL):
                mark = marks[first + step]
                pltpu.store(
                    rows.at[pl.ds(mark >> 4, 1), :],
                    turned[pl.ds(first + step, 1), :],
                    mask=group == (mark & 15),
                )
            return carry

        return lax.fori_loop(0, (counts[o] + UNROLL - 1) // UNROLL, chunk, carry)

    lax.fori_loop(0, owners + 1, scatter, 0)

    def back(q):
        start = pl.multiple_of(q * LANES, LANES)
        turned[pl.ds(start, LANES), :] = rows[pl.ds(start, LANES), :].T

    def back_some(g, carry):
        for step in range(4):
            back(g * 4 + step)
        return carry

    lax.fori_loop(0, FILL_ROWS // LANES // 4, back_some, 0)

    for c in range(NV):
        filled[c, 0:TILE, :] = jnp.zeros((TILE, LANES), jnp.float32)
        for plane, data in (
            (0, behind[c]),
            (1, field[c, 0:ROWS, :]),
            (CELL_PLANES, field[c, size - ROWS : size, :]),
            (CELL_PLANES + 1, ahead[c]),
        ):
            filled[c, TILE + plane * ROWS : TILE + (plane + 1) * ROWS, :] = data
    for edge in (0, size - ROWS):
        fringes[edge : edge + ROWS, :] = jnp.zeros((ROWS, LANES), jnp.float32)

    def merge(tile, carry):
        base = pl.multiple_of(tile * TILE, TILE)
        inner = pl.multiple_of(base + ROWS, TILE)
        flag = turned[pl.ds(base * TILE + NV, TILE, stride=TILE), :]
        fringes[pl.ds(inner, TILE), :] = flag
        for c in range(NV):
            filled[c, pl.ds(pl.multiple_of(inner + ROWS + TILE, TILE), TILE), :] = jnp.where(
                flag > 0.5,
                turned[pl.ds(base * TILE + c, TILE, stride=TILE), :],
                field[c, pl.ds(inner, TILE), :],
            )
        return carry

    lax.fori_loop(0, (CELL_PLANES - 2) * ROWS // TILE, merge, 0)

    def relax(i, carry):
        for part in range(ROWS // TILE):
            base = pl.multiple_of(i * ROWS + part * TILE, TILE)
            here = base + ROWS + TILE
            rate = ratio[pl.ds(base, TILE), :]
            scale = 1.0 / (1.0 + 6.0 * rate)
            fringe = fringes[pl.ds(base, TILE), :] > 0.5
            for c in range(NV):
                mid = filled[c, pl.ds(pl.multiple_of(here, TILE), TILE), :]
                up = filled[c, pl.ds(here + 1, TILE), :]
                down = filled[c, pl.ds(here - 1, TILE), :]
                if part == 0:
                    down = jnp.where(level == 0, 0.0, down)
                if part == ROWS // TILE - 1:
                    up = jnp.where(level == TILE - 1, 0.0, up)
                left = jnp.where(lane == 0, 0.0, pltpu.roll(mid, 1, 1))
                right = jnp.where(lane == LANES - 1, 0.0, pltpu.roll(mid, LANES - 1, 1))
                total = (
                    filled[c, pl.ds(pl.multiple_of(here + ROWS, TILE), TILE), :]
                    + filled[c, pl.ds(pl.multiple_of(here - ROWS, TILE), TILE), :]
                    + up
                    + down
                    + left
                    + right
                )
                out[c, pl.ds(base, TILE), :] = jnp.where(
                    fringe, mid, (mid + rate * total) * scale
                )
        return carry

    lax.fori_loop(0, CELL_PLANES, relax, 0)


def fill_and_relax(marks, counts, values, extra_values, field, behind, ahead, ratio):
    owners = counts.shape[0] - 1
    size = CELL_PLANES * ROWS
    vmem = pl.BlockSpec(memory_space=pltpu.VMEM)
    smem = pl.BlockSpec(memory_space=pltpu.SMEM)
    return pl.pallas_call(
        fill_kernel,
        out_shape=jax.ShapeDtypeStruct(field.shape, jnp.float32),
        in_specs=[smem] * 2 + [vmem] * 6,
        out_specs=vmem,
        scratch_shapes=[
            pltpu.VMEM(((owners + 1) * TILE, LANES), jnp.float32),
            pltpu.VMEM((max((owners + 1) * LANES, FILL_ROWS), LANES), jnp.float32),
            pltpu.VMEM((FILL_ROWS + TILE, LANES), jnp.float32),
            pltpu.VMEM((NV, size + 2 * ROWS + 2 * TILE, LANES), jnp.float32),
            pltpu.VMEM((size, LANES), jnp.float32),
        ],
        compiler_params=pltpu.CompilerParams(vmem_limit_bytes=48 << 20),
        name="fill",
    )(marks, counts, values, extra_values, field, behind, ahead, ratio)


def passed_along(value, axis, steps):
    count = lax.axis_size(axis)
    pairs = [(source, (source + steps) % count) for source in range(count)]
    return lax.ppermute(value, axis, pairs)


def on_device(
    field, node_jitter, time_ratio, donor_cell, receptor_offset, receptor_node, point_count
):
    grids = lax.axis_size("grid")
    ahead = passed_along(jnp.concatenate([field[:, 0], node_jitter[:, 0]], 0), "sub", -1)
    behind = passed_along(field[:, CELL_PLANES - 1], "sub", 1)

    heavy = (lax.axis_index("grid") + 1) % grids
    counts = point_count[0]
    slot = jnp.arange(LANES, dtype=jnp.int32)
    marked = jnp.where(slot[None, :] < counts[:, None], donor_cell[0, :, 0], -1)
    request = jnp.concatenate(
        [marked.astype(jnp.float32)[:, None], receptor_offset[0, :, 0]], 1
    )
    more_cells = lax.dynamic_index_in_dim(donor_cell[0, :, 1], heavy, 0, False)
    more_offsets = lax.dynamic_index_in_dim(receptor_offset[0, :, 1], heavy, 0, False)
    more = jnp.concatenate([more_cells.astype(jnp.float32)[None], more_offsets], 0)

    request = lax.all_to_all(request, "grid", split_axis=0, concat_axis=0, tiled=True)
    more = passed_along(more, "grid", 1)
    cells = jnp.concatenate([request[:, 0], more[:1]], 0).astype(jnp.int32)
    asked = jnp.sum((cells >= 0).astype(jnp.int32), axis=1)
    offsets = jnp.moveaxis(request[:, 1:], 1, 0)
    extra_offsets = jnp.concatenate([more[1:], jnp.zeros((5, LANES), jnp.float32)], 0)

    flat_field = field.reshape(NV, CELL_PLANES * ROWS, LANES)
    values = donor_values(
        jnp.maximum(cells, 0),
        asked,
        flat_field,
        node_jitter.reshape(3, CELL_PLANES * ROWS, LANES),
        ahead,
        offsets,
        extra_offsets,
    )
    answer = values[: grids * TILE].reshape(grids, TILE, LANES)[:, :NV]
    more_answer = values[grids * TILE : (grids + 1) * TILE]
    answer = lax.all_to_all(answer, "grid", split_axis=0, concat_axis=0, tiled=True)
    more_answer = passed_along(more_answer, "grid", -1)

    more_nodes = lax.dynamic_index_in_dim(receptor_node[0, :, 1], heavy, 0, True)
    nodes = jnp.concatenate([receptor_node[0, :, 0], more_nodes], 0)
    live = jnp.concatenate(
        [
            jnp.minimum(counts, LANES),
            lax.dynamic_index_in_dim(counts, heavy, 0, True) - LANES,
        ]
    )
    place = (((nodes >> 11) - 2) << 7) + (nodes & (LANES - 1))
    place = (place << 4) + ((nodes >> 7) & 15)
    marks = jnp.where(slot[None, :] < live[:, None], place, FILL_ROWS << 4)
    out = fill_and_relax(
        marks.reshape(-1),
        live,
        answer,
        more_answer,
        flat_field,
        behind,
        ahead[:NV],
        time_ratio.reshape(CELL_PLANES * ROWS, LANES),
    )
    return out.reshape(field.shape)


def solution(mesh):
    placed = (
        P(None, ("grid", "sub"), None, None),
        P(None, ("grid", "sub"), None, None),
        P(("grid", "sub"), None, None),
        P(("grid", "sub"), None, None, None),
        P(("grid", "sub"), None, None, None, None),
        P(("grid", "sub"), None, None, None),
        P(("grid", "sub"), None),
    )
    return jax.shard_map(
        on_device,
        mesh=mesh,
        in_specs=placed,
        out_specs=P(None, ("grid", "sub"), None, None),
        check_vma=False,
    )
```

```python
import jax
import jax.numpy as jnp
from jax import lax
from jax.experimental import pallas as pl
from jax.experimental.pallas import tpu as pltpu
from jax.sharding import PartitionSpec as P

LANES = 128
TILE = 8
ROWS = 32
CELL_PLANES = 8
PLANE = ROWS * LANES
NV = 5
UNROLL = 16
HALF_CELLS = CELL_PLANES // 2 * PLANE
FILL_ROWS = (CELL_PLANES - 2) * PLANE // 16


def lerp(low, high, weight):
    return low + weight * (high - low)


def solve_group(places, target):
    size = target[0].shape
    param = [jnp.full(size, 0.5, jnp.float32) for _ in range(3)]
    rise = [
        [[places[m][a][b][1] - places[m][a][b][0] for b in range(2)] for a in range(2)]
        for m in range(3)
    ]
    for _ in range(4):
        u, v, w = param
        misfit, jac = [], []
        for m in range(3):
            edge = [[places[m][a][b][0] + w * rise[m][a][b] for b in range(2)] for a in range(2)]
            across = [edge[a][1] - edge[a][0] for a in range(2)]
            face = [edge[a][0] + v * across[a] for a in range(2)]
            slope0 = face[1] - face[0]
            misfit.append(face[0] + u * slope0 - target[m])
            slope1 = lerp(across[0], across[1], u)
            slope2 = lerp(
                lerp(rise[m][0][0], rise[m][0][1], v), lerp(rise[m][1][0], rise[m][1][1], v), u
            )
            jac.append((slope0, slope1, slope2))
        x, y, z = ([jac[m][d] for m in range(3)] for d in range(3))

        def cross(p, q):
            return [
                p[1] * q[2] - p[2] * q[1],
                p[2] * q[0] - p[0] * q[2],
                p[0] * q[1] - p[1] * q[0],
            ]

        def dot(p, q):
            return p[0] * q[0] + p[1] * q[1] + p[2] * q[2]

        yz, zx, xy = cross(y, z), cross(z, x), cross(x, y)
        inverse = 1.0 / dot(x, yz)
        param = [
            u - dot(misfit, yz) * inverse,
            v - dot(misfit, zx) * inverse,
            w - dot(misfit, xy) * inverse,
        ]
    return param


def donor_kernel(
    cells, offsets, field, jitter,
    answers, ahead, behind,
    cells_in, cells_now, offsets_in, field_here, jitter_here, tiles, shifted, table, picked, corners, sent,
    local_sems, halo_send, halo_recv, cell_send, cell_recv, offset_send, offset_recv,
    answer_send, answer_recv,
):
    grids = lax.axis_size("grid")
    subs = lax.axis_size("sub")
    me = lax.axis_index("grid")
    sub = lax.axis_index("sub")
    after, before = lax.rem(me + 1, grids), lax.rem(me + grids - 1, grids)
    sub_after, sub_before = lax.rem(sub + 1, subs), lax.rem(sub + subs - 1, subs)

    barrier = pltpu.get_barrier_semaphore()

    def greet(s, carry):
        pl.semaphore_signal(barrier, inc=1, device_id={"grid": lax.rem(me + s, grids)})
        return carry

    lax.fori_loop(1, grids, greet, 0)
    pl.semaphore_signal(barrier, inc=1, device_id={"sub": sub_after})
    pl.semaphore_signal(barrier, inc=1, device_id={"sub": sub_before})

    loads = [
        pltpu.make_async_copy(field, field_here, local_sems.at[0]),
        pltpu.make_async_copy(jitter, jitter_here, local_sems.at[1]),
    ]
    for load in loads:
        load.start()
    for load in loads:
        load.wait()

    def put(start, data):
        tiles[pl.ds(start, TILE, stride=TILE), :] = data
        shifted[pl.ds(start, TILE, stride=TILE), :] = pltpu.roll(data, LANES - 1, 1)

    def fill(tile, carry):
        base = pl.multiple_of(tile * TILE, TILE)
        for c in range(NV):
            put(base * TILE + c, field_here[c, pl.ds(base, TILE), :])
        for c in range(3):
            put(base * TILE + NV + c, jitter_here[c, pl.ds(base, TILE), :])
        return carry

    lax.fori_loop(0, CELL_PLANES * ROWS // TILE, fill, 0)
    pl.semaphore_wait(barrier, grids + 1)

    def remote(source, target, send, recv, device):
        return pltpu.make_async_remote_copy(
            src_ref=source, dst_ref=target, send_sem=send, recv_sem=recv, device_id=device
        )

    first, last = pl.ds(0, ROWS), pl.ds((CELL_PLANES - 1) * ROWS, ROWS)
    halos = [
        remote(
            field_here.at[:, first], ahead.at[pl.ds(0, NV)],
            halo_send.at[0], halo_recv.at[0], {"sub": sub_before},
        ),
        remote(
            jitter_here.at[:, first], ahead.at[pl.ds(NV, 3)],
            halo_send.at[1], halo_recv.at[1], {"sub": sub_before},
        ),
        remote(
            field_here.at[:, last], behind, halo_send.at[2], halo_recv.at[2], {"sub": sub_after}
        ),
    ]
    for halo in halos:
        halo.start()

    def cell_copy(peer):
        return remote(
            cells.at[peer, 0], cells_in.at[me], cell_send.at[0], cell_recv.at[0], {"grid": peer}
        )

    def offset_copy(peer):
        return remote(
            offsets.at[peer, 0], offsets_in.at[pl.ds(me * TILE, 3)],
            offset_send.at[0], offset_recv.at[0], {"grid": peer},
        )

    def send_cells(s, carry):
        cell_copy(lax.rem(me + s, grids)).start()
        return carry

    def send_offsets(s, carry):
        offset_copy(lax.rem(me + s, grids)).start()
        return carry

    lax.fori_loop(1, grids, send_cells, 0)
    more_cells = remote(
        cells.at[after, 1], cells_in.at[grids], cell_send.at[1], cell_recv.at[1], {"grid": after}
    )
    more_cells.start()
    own_cells = pltpu.make_async_copy(cells.at[me, 0], cells_in.at[me], local_sems.at[0])
    own_cells.start()
    lax.fori_loop(1, grids, send_offsets, 0)
    more_offsets = remote(
        offsets.at[after, 1], offsets_in.at[pl.ds(grids * TILE, 3)],
        offset_send.at[1], offset_recv.at[1], {"grid": after},
    )
    more_offsets.start()
    own_offsets = pltpu.make_async_copy(
        offsets.at[me, 0], offsets_in.at[pl.ds(me * TILE, 3)], local_sems.at[1]
    )
    own_offsets.start()

    def build_some(q, carry):
        for step in range(4):
            row = q * 4 + step
            parts = []
            for half in range(2):
                for a in (0, 1, ROWS, ROWS + 1):
                    start = (row + half * (CELL_PLANES // 2) * ROWS + a) * TILE
                    start = pl.multiple_of(start, TILE)
                    parts.append(tiles[pl.ds(start, TILE), :])
                    parts.append(shifted[pl.ds(start, TILE), :])
            table[pl.ds(pl.multiple_of(row * LANES, LANES), LANES), :] = jnp.concatenate(
                parts, 0
            ).T
        return carry

    quarter = ROWS // 4
    lax.fori_loop(0, 3 * quarter, build_some, 0)
    halos[0].wait_recv()
    halos[1].wait_recv()
    for tile in range(ROWS // TILE):
        for c in range(8):
            put(
                (CELL_PLANES * ROWS + tile * TILE) * TILE + c,
                ahead[c, pl.ds(tile * TILE, TILE), :],
            )

    def drain(buffer, sem):
        pltpu.make_async_copy(buffer, buffer, sem).wait()

    drain(cells_in.at[pl.ds(0, grids - 1)], cell_recv.at[0])
    own_cells.wait()
    more_cells.wait_recv()
    load_cells = pltpu.make_async_copy(cells_in, cells_now, local_sems.at[0])
    load_cells.start()
    lax.fori_loop(3 * quarter, 4 * quarter, build_some, 0)
    load_cells.wait()
    drain(picked.at[pl.ds(0, 3 * (grids - 1))], offset_recv.at[0])
    own_offsets.wait()
    more_offsets.wait_recv()

    def pick(block, count):
        def chunk(q, carry):
            b = block + q // (LANES // UNROLL)
            t = lax.rem(q, LANES // UNROLL) * UNROLL
            to = pl.multiple_of(q * UNROLL, UNROLL)
            for step in range(UNROLL):
                row = cells_now[b, t + step] & (HALF_CELLS - 1)
                picked[pl.ds(to + step, 1), :] = table[pl.ds(row, 1), :]
            return carry

        lax.fori_loop(0, count * (LANES // UNROLL), chunk, 0)

    def turn(block, r):
        values = picked[r * LANES : (r + 1) * LANES, :].T
        far = cells_in[pl.ds(block + r, 1), :] >= HALF_CELLS
        for q in range(8):
            corners[q, r * TILE : (r + 1) * TILE, :] = jnp.where(
                far, values[64 + 8 * q : 72 + 8 * q], values[8 * q : 8 * q + 8]
            )

    def solve(block):
        target = [
            offsets_in[pl.ds(block * TILE + m, TILE, stride=TILE), :] for m in range(3)
        ]
        places = [
            [
                [
                    [
                        corners[4 * a + 2 * b + d, pl.ds(NV + m, TILE, stride=TILE), :]
                        + float((a, b, d)[m])
                        for d in range(2)
                    ]
                    for b in range(2)
                ]
                for a in range(2)
            ]
            for m in range(3)
        ]
        u, v, w = solve_group(places, target)
        for c in range(NV):
            node = [corners[q, pl.ds(c, TILE, stride=TILE), :] for q in range(8)]
            edge = [lerp(node[2 * e], node[2 * e + 1], w) for e in range(4)]
            value = lerp(lerp(edge[0], edge[1], v), lerp(edge[2], edge[3], v), u)
            sent[pl.ds(block * TILE + c, TILE, stride=TILE), :] = value

    own_answer = pltpu.make_async_copy(
        sent.at[pl.ds(me * TILE, NV)], answers.at[pl.ds(me * TILE, NV)], local_sems.at[0]
    )

    def group(g, carry):
        block = pl.multiple_of(lax.rem(me // TILE + g, grids // TILE) * TILE, TILE)
        pick(block, TILE)
        for r in range(TILE):
            turn(block, r)
        solve(block)

        def answer(r, carry):
            peer = block + r

            @pl.when(peer != me)
            def _():
                remote(
                    sent.at[pl.ds(peer * TILE, NV)], answers.at[pl.ds(me * TILE, NV)],
                    answer_send.at[0], answer_recv.at[0], {"grid": peer},
                ).start()

            @pl.when(peer == me)
            def _():
                own_answer.start()

            return carry

        lax.fori_loop(0, TILE, answer, 0)
        return carry

    lax.fori_loop(0, grids // TILE, group, 0)
    pick(grids, 1)
    turn(grids, 0)
    solve(grids)
    more_answers = remote(
        sent.at[pl.ds(grids * TILE, NV)], answers.at[pl.ds(grids * TILE, NV)],
        answer_send.at[1], answer_recv.at[1], {"grid": before},
    )
    more_answers.start()

    drain(picked.at[pl.ds(0, NV * (grids - 1))], answer_recv.at[0])
    own_answer.wait()
    more_answers.wait()
    drain(picked.at[pl.ds(0, NV * (grids - 1))], answer_send.at[0])
    drain(cells_in.at[pl.ds(0, grids - 1)], cell_send.at[0])
    drain(picked.at[pl.ds(0, 3 * (grids - 1))], offset_send.at[0])
    more_cells.wait_send()
    more_offsets.wait_send()
    for halo in halos:
        halo.wait_send()
    halos[2].wait_recv()


def donor_values(cells, offsets, field, jitter):
    grids = cells.shape[0]
    padded = grids + TILE
    node_rows = (CELL_PLANES + 1) * ROWS
    vmem = pl.BlockSpec(memory_space=pltpu.VMEM)
    anywhere = pl.BlockSpec(memory_space=pl.ANY)
    f32 = jnp.float32
    return pl.pallas_call(
        donor_kernel,
        out_shape=(
            jax.ShapeDtypeStruct(((grids + 1) * TILE, LANES), f32),
            jax.ShapeDtypeStruct((8, ROWS, LANES), f32),
            jax.ShapeDtypeStruct((NV, ROWS, LANES), f32),
        ),
        in_specs=[anywhere] * 4,
        out_specs=(vmem,) * 3,
        scratch_shapes=[
            pltpu.VMEM((padded, LANES), jnp.int32),
            pltpu.SMEM((padded, LANES), jnp.int32),
            pltpu.VMEM((padded * TILE, LANES), f32),
            pltpu.VMEM(field.shape, f32),
            pltpu.VMEM(jitter.shape, f32),
            pltpu.VMEM((node_rows * TILE + 2 * TILE, LANES), f32),
            pltpu.VMEM((node_rows * TILE + 2 * TILE, LANES), f32),
            pltpu.VMEM((HALF_CELLS, LANES), f32),
            pltpu.VMEM((TILE * LANES, LANES), f32),
            pltpu.VMEM((8, TILE * TILE, LANES), f32),
            pltpu.VMEM((padded * TILE, LANES), f32),
        ]
        + [pltpu.SemaphoreType.DMA((n,)) for n in (2, 3, 3, 2, 2, 2, 2, 2, 2)],
        compiler_params=pltpu.CompilerParams(
            collective_id=0, has_side_effects=True, vmem_limit_bytes=48 << 20
        ),
        name="donor",
    )(cells, offsets, field, jitter)


def fill_kernel(
    marks, counts, values, field, behind, ahead, ratio, out,
    turned, rows, filled, fringes,
):
    owners = counts.shape[0] - 1
    size = CELL_PLANES * ROWS
    group = lax.broadcasted_iota(jnp.int32, (1, LANES), 1) >> 3
    lane = lax.broadcasted_iota(jnp.int32, (TILE, LANES), 1)
    level = lax.broadcasted_iota(jnp.int32, (TILE, LANES), 0)

    def clear(q, carry):
        rows[pl.ds(pl.multiple_of(q * LANES, LANES), LANES), :] = jnp.zeros(
            (LANES, LANES), jnp.float32
        )
        return carry

    lax.fori_loop(0, FILL_ROWS // LANES, clear, 0)

    def spread(o):
        block = values[pl.ds(pl.multiple_of(o * TILE, TILE), TILE), :]
        block = jnp.where(level < NV, block, 1.0)
        start = pl.multiple_of(o * LANES, LANES)
        turned[pl.ds(start, LANES), :] = jnp.concatenate([block] * 16, 0).T

    def spread_some(g, carry):
        for step in range(4):
            spread(g * 4 + step)
        return carry

    lax.fori_loop(0, owners // 4, spread_some, 0)
    spread(owners)

    def scatter(o, carry):
        def chunk(q, carry):
            first = pl.multiple_of(o * LANES + q * UNROLL, UNROLL)
            for step in range(UNROLL):
                mark = marks[first + step]
                pltpu.store(
                    rows.at[pl.ds(mark >> 4, 1), :],
                    turned[pl.ds(first + step, 1), :],
                    mask=group == (mark & 15),
                )
            return carry

        return lax.fori_loop(0, (counts[o] + UNROLL - 1) // UNROLL, chunk, carry)

    lax.fori_loop(0, owners + 1, scatter, 0)

    def back(q):
        start = pl.multiple_of(q * LANES, LANES)
        turned[pl.ds(start, LANES), :] = rows[pl.ds(start, LANES), :].T

    def back_some(g, carry):
        for step in range(4):
            back(g * 4 + step)
        return carry

    lax.fori_loop(0, FILL_ROWS // LANES // 4, back_some, 0)

    for c in range(NV):
        filled[c, 0:TILE, :] = jnp.zeros((TILE, LANES), jnp.float32)
        for plane, data in (
            (0, behind[c]),
            (1, field[c, 0:ROWS, :]),
            (CELL_PLANES, field[c, size - ROWS : size, :]),
            (CELL_PLANES + 1, ahead[c]),
        ):
            filled[c, TILE + plane * ROWS : TILE + (plane + 1) * ROWS, :] = data
    for edge in (0, size - ROWS):
        fringes[edge : edge + ROWS, :] = jnp.zeros((ROWS, LANES), jnp.float32)

    def merge(tile, carry):
        base = pl.multiple_of(tile * TILE, TILE)
        inner = pl.multiple_of(base + ROWS, TILE)
        flag = turned[pl.ds(base * TILE + NV, TILE, stride=TILE), :]
        fringes[pl.ds(inner, TILE), :] = flag
        for c in range(NV):
            filled[c, pl.ds(pl.multiple_of(inner + ROWS + TILE, TILE), TILE), :] = jnp.where(
                flag > 0.5,
                turned[pl.ds(base * TILE + c, TILE, stride=TILE), :],
                field[c, pl.ds(inner, TILE), :],
            )
        return carry

    lax.fori_loop(0, (CELL_PLANES - 2) * ROWS // TILE, merge, 0)

    def relax(i, carry):
        for part in range(ROWS // TILE):
            base = pl.multiple_of(i * ROWS + part * TILE, TILE)
            here = base + ROWS + TILE
            rate = ratio[pl.ds(base, TILE), :]
            scale = 1.0 / (1.0 + 6.0 * rate)
            fringe = fringes[pl.ds(base, TILE), :] > 0.5
            for c in range(NV):
                mid = filled[c, pl.ds(pl.multiple_of(here, TILE), TILE), :]
                up = filled[c, pl.ds(here + 1, TILE), :]
                down = filled[c, pl.ds(here - 1, TILE), :]
                if part == 0:
                    down = jnp.where(level == 0, 0.0, down)
                if part == ROWS // TILE - 1:
                    up = jnp.where(level == TILE - 1, 0.0, up)
                left = jnp.where(lane == 0, 0.0, pltpu.roll(mid, 1, 1))
                right = jnp.where(lane == LANES - 1, 0.0, pltpu.roll(mid, LANES - 1, 1))
                total = (
                    filled[c, pl.ds(pl.multiple_of(here + ROWS, TILE), TILE), :]
                    + filled[c, pl.ds(pl.multiple_of(here - ROWS, TILE), TILE), :]
                    + up
                    + down
                    + left
                    + right
                )
                out[c, pl.ds(base, TILE), :] = jnp.where(
                    fringe, mid, (mid + rate * total) * scale
                )
        return carry

    lax.fori_loop(0, CELL_PLANES, relax, 0)


def fill_and_relax(marks, counts, values, field, behind, ahead, ratio):
    owners = counts.shape[0] - 1
    size = CELL_PLANES * ROWS
    vmem = pl.BlockSpec(memory_space=pltpu.VMEM)
    smem = pl.BlockSpec(memory_space=pltpu.SMEM)
    return pl.pallas_call(
        fill_kernel,
        out_shape=jax.ShapeDtypeStruct(field.shape, jnp.float32),
        in_specs=[smem] * 2 + [vmem] * 5,
        out_specs=vmem,
        scratch_shapes=[
            pltpu.VMEM((max((owners + 1) * LANES, FILL_ROWS), LANES), jnp.float32),
            pltpu.VMEM((FILL_ROWS + TILE, LANES), jnp.float32),
            pltpu.VMEM((NV, size + 2 * ROWS + 2 * TILE, LANES), jnp.float32),
            pltpu.VMEM((size, LANES), jnp.float32),
        ],
        compiler_params=pltpu.CompilerParams(vmem_limit_bytes=48 << 20),
        name="fill",
    )(marks, counts, values, field, behind, ahead, ratio)


def on_device(
    field, node_jitter, time_ratio, donor_cell, receptor_offset, receptor_node, point_count
):
    grids = lax.axis_size("grid")
    heavy = (lax.axis_index("grid") + 1) % grids
    flat_field = field.reshape(NV, CELL_PLANES * ROWS, LANES)
    answers, ahead, behind = donor_values(
        donor_cell[0],
        receptor_offset[0],
        flat_field,
        node_jitter.reshape(3, CELL_PLANES * ROWS, LANES),
    )

    counts = point_count[0]
    slot = jnp.arange(LANES, dtype=jnp.int32)
    more_nodes = lax.dynamic_index_in_dim(receptor_node[0, :, 1], heavy, 0, True)
    nodes = jnp.concatenate([receptor_node[0, :, 0], more_nodes], 0)
    live = jnp.concatenate(
        [
            jnp.minimum(counts, LANES),
            lax.dynamic_index_in_dim(counts, heavy, 0, True) - LANES,
        ]
    )
    place = (((nodes >> 11) - 2) << 7) + (nodes & (LANES - 1))
    place = (place << 4) + ((nodes >> 7) & 15)
    marks = jnp.where(slot[None, :] < live[:, None], place, FILL_ROWS << 4)
    out = fill_and_relax(
        marks.reshape(-1),
        live,
        answers,
        flat_field,
        behind,
        ahead,
        time_ratio.reshape(CELL_PLANES * ROWS, LANES),
    )
    return out.reshape(field.shape)


def solution(mesh):
    placed = (
        P(None, ("grid", "sub"), None, None),
        P(None, ("grid", "sub"), None, None),
        P(("grid", "sub"), None, None),
        P(("grid", "sub"), None, None, None),
        P(("grid", "sub"), None, None, None, None),
        P(("grid", "sub"), None, None, None),
        P(("grid", "sub"), None),
    )
    return jax.shard_map(
        on_device,
        mesh=mesh,
        in_specs=placed,
        out_specs=P(None, ("grid", "sub"), None, None),
        check_vma=False,
    )
```

```python
import jax
import jax.numpy as jnp
from jax import lax
from jax.experimental import pallas as pl
from jax.experimental.pallas import tpu as pltpu
from jax.sharding import PartitionSpec as P

LANES = 128
TILE = 8
ROWS = 32
CELL_PLANES = 8
PLANE = ROWS * LANES
NV = 5
UNROLL = 16
HALF_CELLS = CELL_PLANES // 2 * PLANE
FILL_ROWS = (CELL_PLANES - 2) * PLANE // 16


def lerp(low, high, weight):
    return low + weight * (high - low)


def solve_group(places, target):
    size = target[0].shape
    param = [jnp.full(size, 0.5, jnp.float32) for _ in range(3)]
    rise = [
        [[places[m][a][b][1] - places[m][a][b][0] for b in range(2)] for a in range(2)]
        for m in range(3)
    ]
    for _ in range(4):
        u, v, w = param
        misfit, jac = [], []
        for m in range(3):
            edge = [[places[m][a][b][0] + w * rise[m][a][b] for b in range(2)] for a in range(2)]
            across = [edge[a][1] - edge[a][0] for a in range(2)]
            face = [edge[a][0] + v * across[a] for a in range(2)]
            slope0 = face[1] - face[0]
            misfit.append(face[0] + u * slope0 - target[m])
            slope1 = lerp(across[0], across[1], u)
            slope2 = lerp(
                lerp(rise[m][0][0], rise[m][0][1], v), lerp(rise[m][1][0], rise[m][1][1], v), u
            )
            jac.append((slope0, slope1, slope2))
        x, y, z = ([jac[m][d] for m in range(3)] for d in range(3))

        def cross(p, q):
            return [
                p[1] * q[2] - p[2] * q[1],
                p[2] * q[0] - p[0] * q[2],
                p[0] * q[1] - p[1] * q[0],
            ]

        def dot(p, q):
            return p[0] * q[0] + p[1] * q[1] + p[2] * q[2]

        yz, zx, xy = cross(y, z), cross(z, x), cross(x, y)
        inverse = 1.0 / dot(x, yz)
        param = [
            u - dot(misfit, yz) * inverse,
            v - dot(misfit, zx) * inverse,
            w - dot(misfit, xy) * inverse,
        ]
    return param


def donor_kernel(
    cells, offsets, field, jitter, nodes, counts,
    answers, ahead_out, behind_out, mark_rows_out, mark_groups_out,
    ahead, behind, mark_rows, mark_groups, counts_now, cells_in, cells_near, cells_now, offsets_in, field_here, jitter_here, tiles, shifted, table, picked, corners, sent,
    local_sems, halo_send, halo_recv, cell_send, cell_recv, offset_send, offset_recv,
    answer_send, answer_recv,
):
    grids = lax.axis_size("grid")
    subs = lax.axis_size("sub")
    me = lax.axis_index("grid")
    sub = lax.axis_index("sub")
    after, before = lax.rem(me + 1, grids), lax.rem(me + grids - 1, grids)
    sub_after, sub_before = lax.rem(sub + 1, subs), lax.rem(sub + subs - 1, subs)

    barrier = pltpu.get_barrier_semaphore()

    def greet(s, carry):
        pl.semaphore_signal(barrier, inc=1, device_id={"grid": lax.rem(me + s, grids)})
        return carry

    lax.fori_loop(1, grids, greet, 0)
    pl.semaphore_signal(barrier, inc=1, device_id={"sub": sub_after})
    pl.semaphore_signal(barrier, inc=1, device_id={"sub": sub_before})

    loads = [
        pltpu.make_async_copy(field, field_here, local_sems.at[0]),
        pltpu.make_async_copy(jitter, jitter_here, local_sems.at[1]),
    ]
    side_loads = [
        pltpu.make_async_copy(counts.at[0], counts_now, local_sems.at[2]),
        pltpu.make_async_copy(nodes.at[:, 0], mark_rows.at[pl.ds(0, grids)], local_sems.at[3]),
        pltpu.make_async_copy(nodes.at[after, 1], mark_rows.at[grids], local_sems.at[4]),
    ]
    for load in loads + side_loads:
        load.start()
    for load in loads:
        load.wait()

    def put(start, data):
        tiles[pl.ds(start, TILE, stride=TILE), :] = data
        shifted[pl.ds(start, TILE, stride=TILE), :] = pltpu.roll(data, LANES - 1, 1)

    def fill(tile, carry):
        base = pl.multiple_of(tile * TILE, TILE)
        for c in range(NV):
            put(base * TILE + c, field_here[c, pl.ds(base, TILE), :])
        for c in range(3):
            put(base * TILE + NV + c, jitter_here[c, pl.ds(base, TILE), :])
        return carry

    lax.fori_loop(0, CELL_PLANES * ROWS // TILE, fill, 0)
    pl.semaphore_wait(barrier, grids + 1)

    def remote(source, target, send, recv, device):
        return pltpu.make_async_remote_copy(
            src_ref=source, dst_ref=target, send_sem=send, recv_sem=recv, device_id=device
        )

    first, last = pl.ds(0, ROWS), pl.ds((CELL_PLANES - 1) * ROWS, ROWS)
    halos = [
        remote(
            field_here.at[:, first], ahead.at[pl.ds(0, NV)],
            halo_send.at[0], halo_recv.at[0], {"sub": sub_before},
        ),
        remote(
            jitter_here.at[:, first], ahead.at[pl.ds(NV, 3)],
            halo_send.at[1], halo_recv.at[1], {"sub": sub_before},
        ),
        remote(
            field_here.at[:, last], behind, halo_send.at[2], halo_recv.at[2], {"sub": sub_after}
        ),
    ]
    for halo in halos:
        halo.start()

    def cell_copy(peer):
        return remote(
            cells.at[peer, 0], cells_in.at[me], cell_send.at[0], cell_recv.at[0], {"grid": peer}
        )

    def offset_copy(peer):
        return remote(
            offsets.at[peer, :, 0], offsets_in.at[pl.ds(me * TILE, 3)],
            offset_send.at[0], offset_recv.at[0], {"grid": peer},
        )

    def send_cells(s, carry):
        cell_copy(lax.rem(me + s, grids)).start()
        return carry

    def send_offsets(s, carry):
        offset_copy(lax.rem(me + s, grids)).start()
        return carry

    lax.fori_loop(1, grids, send_cells, 0)
    more_cells = remote(
        cells.at[after, 1], cells_in.at[grids], cell_send.at[1], cell_recv.at[1], {"grid": after}
    )
    more_cells.start()
    own_cells = pltpu.make_async_copy(cells.at[me, 0], cells_in.at[me], local_sems.at[0])
    own_cells.start()
    lax.fori_loop(1, grids, send_offsets, 0)
    more_offsets = remote(
        offsets.at[after, :, 1], offsets_in.at[pl.ds(grids * TILE, 3)],
        offset_send.at[1], offset_recv.at[1], {"grid": after},
    )
    more_offsets.start()
    own_offsets = pltpu.make_async_copy(
        offsets.at[me, :, 0], offsets_in.at[pl.ds(me * TILE, 3)], local_sems.at[1]
    )
    own_offsets.start()

    for load in side_loads:
        load.wait()
    slot = lax.broadcasted_iota(jnp.int32, (1, LANES), 1)

    def mark(o, live):
        node = mark_rows[pl.ds(o, 1), :]
        place = (((node >> 11) - 2) << 7) + (node & (LANES - 1))
        mark_rows[pl.ds(o, 1), :] = jnp.where(slot < live, place, FILL_ROWS)
        mark_groups[pl.ds(o, 1), :] = (node >> 7) & 15

    def mark_step(o, carry):
        mark(o, counts_now[o])
        return carry

    lax.fori_loop(0, grids, mark_step, 0)
    mark(grids, counts_now[after] - LANES)
    stores = [
        pltpu.make_async_copy(mark_rows, mark_rows_out, local_sems.at[3]),
        pltpu.make_async_copy(mark_groups, mark_groups_out, local_sems.at[4]),
        pltpu.make_async_copy(ahead, ahead_out, local_sems.at[5]),
        pltpu.make_async_copy(behind, behind_out, local_sems.at[6]),
    ]
    stores[0].start()
    stores[1].start()

    def build_some(q, carry):
        for step in range(4):
            row = q * 4 + step
            parts = []
            for half in range(2):
                for a in (0, 1, ROWS, ROWS + 1):
                    start = (row + half * (CELL_PLANES // 2) * ROWS + a) * TILE
                    start = pl.multiple_of(start, TILE)
                    parts.append(tiles[pl.ds(start, TILE), :])
                    parts.append(shifted[pl.ds(start, TILE), :])
            table[pl.ds(pl.multiple_of(row * LANES, LANES), LANES), :] = jnp.concatenate(
                parts, 0
            ).T
        return carry

    quarter = ROWS // 4
    lax.fori_loop(0, 3 * quarter, build_some, 0)
    for halo in halos:
        halo.wait_recv()
    stores[2].start()
    stores[3].start()
    for tile in range(ROWS // TILE):
        for c in range(8):
            put(
                (CELL_PLANES * ROWS + tile * TILE) * TILE + c,
                ahead[c, pl.ds(tile * TILE, TILE), :],
            )

    def drain(buffer, sem):
        pltpu.make_async_copy(buffer, buffer, sem).wait()

    drain(cells_in.at[pl.ds(0, grids - 1)], cell_recv.at[0])
    own_cells.wait()
    more_cells.wait_recv()
    cells_near[...] = cells_in[...] & (HALF_CELLS - 1)
    load_cells = pltpu.make_async_copy(cells_near, cells_now, local_sems.at[0])
    load_cells.start()
    lax.fori_loop(3 * quarter, 4 * quarter, build_some, 0)
    load_cells.wait()
    drain(picked.at[pl.ds(0, 3 * (grids - 1))], offset_recv.at[0])
    own_offsets.wait()
    more_offsets.wait_recv()

    def pick(block, count):
        def one(r, carry):
            to = pl.multiple_of(r * LANES, LANES)
            for t in range(LANES):
                picked[pl.ds(to + t, 1), :] = table[pl.ds(cells_now[block + r, t], 1), :]
            return carry

        lax.fori_loop(0, count, one, 0)

    def turn(block, r):
        values = picked[r * LANES : (r + 1) * LANES, :].T
        far = cells_in[pl.ds(block + r, 1), :] >= HALF_CELLS
        for q in range(8):
            corners[q, r * TILE : (r + 1) * TILE, :] = jnp.where(
                far, values[64 + 8 * q : 72 + 8 * q], values[8 * q : 8 * q + 8]
            )

    def solve(block):
        target = [
            offsets_in[pl.ds(block * TILE + m, TILE, stride=TILE), :] for m in range(3)
        ]
        places = [
            [
                [
                    [
                        corners[4 * a + 2 * b + d, pl.ds(NV + m, TILE, stride=TILE), :]
                        + float((a, b, d)[m])
                        for d in range(2)
                    ]
                    for b in range(2)
                ]
                for a in range(2)
            ]
            for m in range(3)
        ]
        u, v, w = solve_group(places, target)
        for c in range(NV):
            node = [corners[q, pl.ds(c, TILE, stride=TILE), :] for q in range(8)]
            edge = [lerp(node[2 * e], node[2 * e + 1], w) for e in range(4)]
            value = lerp(lerp(edge[0], edge[1], v), lerp(edge[2], edge[3], v), u)
            sent[pl.ds(block * TILE + c, TILE, stride=TILE), :] = value

    own_answer = pltpu.make_async_copy(
        sent.at[pl.ds(me * TILE, NV)], answers.at[pl.ds(me * TILE, NV)], local_sems.at[0]
    )

    def group(g, carry):
        block = pl.multiple_of(lax.rem(me // TILE + g, grids // TILE) * TILE, TILE)
        pick(block, TILE)
        for r in range(TILE):
            turn(block, r)
        solve(block)

        def answer(r, carry):
            peer = block + r

            @pl.when(peer != me)
            def _():
                remote(
                    sent.at[pl.ds(peer * TILE, NV)], answers.at[pl.ds(me * TILE, NV)],
                    answer_send.at[0], answer_recv.at[0], {"grid": peer},
                ).start()

            @pl.when(peer == me)
            def _():
                own_answer.start()

            return carry

        lax.fori_loop(0, TILE, answer, 0)
        return carry

    lax.fori_loop(0, grids // TILE, group, 0)
    pick(grids, 1)
    turn(grids, 0)
    solve(grids)
    more_answers = remote(
        sent.at[pl.ds(grids * TILE, NV)], answers.at[pl.ds(grids * TILE, NV)],
        answer_send.at[1], answer_recv.at[1], {"grid": before},
    )
    more_answers.start()

    drain(picked.at[pl.ds(0, NV * (grids - 1))], answer_recv.at[0])
    own_answer.wait()
    more_answers.wait()
    drain(picked.at[pl.ds(0, NV * (grids - 1))], answer_send.at[0])
    drain(cells_in.at[pl.ds(0, grids - 1)], cell_send.at[0])
    drain(picked.at[pl.ds(0, 3 * (grids - 1))], offset_send.at[0])
    more_cells.wait_send()
    more_offsets.wait_send()
    for halo in halos:
        halo.wait_send()
    for store in stores:
        store.wait()


def donor_values(cells, offsets, field, jitter, nodes, counts):
    grids = cells.shape[0]
    padded = grids + TILE
    node_rows = (CELL_PLANES + 1) * ROWS
    hbm = pl.BlockSpec(memory_space=pltpu.HBM)
    f32 = jnp.float32
    return pl.pallas_call(
        donor_kernel,
        out_shape=(
            jax.ShapeDtypeStruct(((grids + 1) * TILE, LANES), f32),
            jax.ShapeDtypeStruct((8, ROWS, LANES), f32),
            jax.ShapeDtypeStruct((NV, ROWS, LANES), f32),
            jax.ShapeDtypeStruct((padded, LANES), jnp.int32),
            jax.ShapeDtypeStruct((padded, LANES), jnp.int32),
        ),
        in_specs=[hbm] * 6,
        out_specs=(hbm,) * 5,
        scratch_shapes=[
            pltpu.VMEM((8, ROWS, LANES), f32),
            pltpu.VMEM((NV, ROWS, LANES), f32),
            pltpu.VMEM((padded, LANES), jnp.int32),
            pltpu.VMEM((padded, LANES), jnp.int32),
            pltpu.SMEM((grids,), jnp.int32),
            pltpu.VMEM((padded, LANES), jnp.int32),
            pltpu.VMEM((padded, LANES), jnp.int32),
            pltpu.SMEM((padded, LANES), jnp.int32),
            pltpu.VMEM((padded * TILE, LANES), f32),
            pltpu.VMEM(field.shape, f32),
            pltpu.VMEM(jitter.shape, f32),
            pltpu.VMEM((node_rows * TILE + 2 * TILE, LANES), f32),
            pltpu.VMEM((node_rows * TILE + 2 * TILE, LANES), f32),
            pltpu.VMEM((HALF_CELLS, LANES), f32),
            pltpu.VMEM((TILE * LANES, LANES), f32),
            pltpu.VMEM((8, TILE * TILE, LANES), f32),
            pltpu.VMEM((padded * TILE, LANES), f32),
        ]
        + [pltpu.SemaphoreType.DMA((n,)) for n in (7, 3, 3, 2, 2, 2, 2, 2, 2)],
        compiler_params=pltpu.CompilerParams(
            collective_id=0, has_side_effects=True, vmem_limit_bytes=60 << 20
        ),
        name="donor",
    )(cells, offsets, field, jitter, nodes, counts)


def fill_kernel(
    counts_in, mark_rows_in, mark_groups_in, values_in, field_in, behind_in, ahead_in, ratio_in, out,
    counts, mark_rows, mark_groups, values, field, behind, ahead, ratio,
    turned, rows, filled, fringes, sems,
):
    owners = counts.shape[0]
    loads = [
        pltpu.make_async_copy(source, target, sems.at[n])
        for n, (source, target) in enumerate(
            (
                (values_in, values),
                (mark_rows_in, mark_rows),
                (mark_groups_in, mark_groups),
                (counts_in.at[0], counts),
                (field_in, field),
                (behind_in, behind),
                (ahead_in, ahead),
                (ratio_in, ratio),
            )
        )
    ]
    for load in loads:
        load.start()
    size = CELL_PLANES * ROWS
    group = lax.broadcasted_iota(jnp.int32, (1, LANES), 1) >> 3
    lane = lax.broadcasted_iota(jnp.int32, (TILE, LANES), 1)
    level = lax.broadcasted_iota(jnp.int32, (TILE, LANES), 0)

    def clear(q, carry):
        rows[pl.ds(pl.multiple_of(q * LANES, LANES), LANES), :] = jnp.zeros(
            (LANES, LANES), jnp.float32
        )
        return carry

    lax.fori_loop(0, FILL_ROWS // LANES, clear, 0)
    loads[0].wait()

    def spread(o):
        block = values[pl.ds(pl.multiple_of(o * TILE, TILE), TILE), :]
        block = jnp.where(level < NV, block, 1.0)
        start = pl.multiple_of(o * LANES, LANES)
        turned[pl.ds(start, LANES), :] = jnp.concatenate([block] * 16, 0).T

    def spread_some(g, carry):
        for step in range(4):
            spread(g * 4 + step)
        return carry

    lax.fori_loop(0, owners // 4, spread_some, 0)
    spread(owners)

    for load in loads[1:4]:
        load.wait()

    def scatter(o, live):
        def chunk(q, carry):
            first = pl.multiple_of(o * LANES + q * UNROLL, UNROLL)
            for step in range(UNROLL):
                t = q * UNROLL + step
                pltpu.store(
                    rows.at[pl.ds(mark_rows[o, t], 1), :],
                    turned[pl.ds(first + step, 1), :],
                    mask=group == mark_groups[o, t],
                )
            return carry

        lax.fori_loop(0, (live + UNROLL - 1) // UNROLL, chunk, 0)

    def scatter_step(o, carry):
        scatter(o, jnp.minimum(counts[o], LANES))
        return carry

    lax.fori_loop(0, owners, scatter_step, 0)
    scatter(owners, LANES)

    def back(q):
        start = pl.multiple_of(q * LANES, LANES)
        turned[pl.ds(start, LANES), :] = rows[pl.ds(start, LANES), :].T

    def back_some(g, carry):
        for step in range(4):
            back(g * 4 + step)
        return carry

    lax.fori_loop(0, FILL_ROWS // LANES // 4, back_some, 0)

    for load in loads[4:]:
        load.wait()

    for c in range(NV):
        filled[c, 0:TILE, :] = jnp.zeros((TILE, LANES), jnp.float32)
        for plane, data in (
            (0, behind[c]),
            (1, field[c, 0:ROWS, :]),
            (CELL_PLANES, field[c, size - ROWS : size, :]),
            (CELL_PLANES + 1, ahead[c]),
        ):
            filled[c, TILE + plane * ROWS : TILE + (plane + 1) * ROWS, :] = data
    for edge in (0, size - ROWS):
        fringes[edge : edge + ROWS, :] = jnp.zeros((ROWS, LANES), jnp.float32)

    def merge(tile, carry):
        base = pl.multiple_of(tile * TILE, TILE)
        inner = pl.multiple_of(base + ROWS, TILE)
        flag = turned[pl.ds(base * TILE + NV, TILE, stride=TILE), :]
        fringes[pl.ds(inner, TILE), :] = flag
        for c in range(NV):
            filled[c, pl.ds(pl.multiple_of(inner + ROWS + TILE, TILE), TILE), :] = jnp.where(
                flag > 0.5,
                turned[pl.ds(base * TILE + c, TILE, stride=TILE), :],
                field[c, pl.ds(inner, TILE), :],
            )
        return carry

    lax.fori_loop(0, (CELL_PLANES - 2) * ROWS // TILE, merge, 0)

    def relax(i, carry):
        for part in range(ROWS // TILE):
            base = pl.multiple_of(i * ROWS + part * TILE, TILE)
            here = base + ROWS + TILE
            rate = ratio[pl.ds(base, TILE), :]
            scale = 1.0 / (1.0 + 6.0 * rate)
            fringe = fringes[pl.ds(base, TILE), :] > 0.5
            for c in range(NV):
                mid = filled[c, pl.ds(pl.multiple_of(here, TILE), TILE), :]
                up = filled[c, pl.ds(here + 1, TILE), :]
                down = filled[c, pl.ds(here - 1, TILE), :]
                if part == 0:
                    down = jnp.where(level == 0, 0.0, down)
                if part == ROWS // TILE - 1:
                    up = jnp.where(level == TILE - 1, 0.0, up)
                left = jnp.where(lane == 0, 0.0, pltpu.roll(mid, 1, 1))
                right = jnp.where(lane == LANES - 1, 0.0, pltpu.roll(mid, LANES - 1, 1))
                total = (
                    filled[c, pl.ds(pl.multiple_of(here + ROWS, TILE), TILE), :]
                    + filled[c, pl.ds(pl.multiple_of(here - ROWS, TILE), TILE), :]
                    + up
                    + down
                    + left
                    + right
                )
                out[c, pl.ds(base, TILE), :] = jnp.where(
                    fringe, mid, (mid + rate * total) * scale
                )
        return carry

    lax.fori_loop(0, CELL_PLANES, relax, 0)


def fill_and_relax(counts, mark_rows, mark_groups, values, field, behind, ahead, ratio):
    owners = counts.shape[1]
    size = CELL_PLANES * ROWS
    hbm = pl.BlockSpec(memory_space=pltpu.HBM)
    f32 = jnp.float32
    return pl.pallas_call(
        fill_kernel,
        out_shape=jax.ShapeDtypeStruct(field.shape, f32),
        in_specs=[hbm] * 8,
        out_specs=pl.BlockSpec(memory_space=pltpu.VMEM),
        scratch_shapes=[
            pltpu.SMEM((owners,), jnp.int32),
            pltpu.SMEM(mark_rows.shape, jnp.int32),
            pltpu.SMEM(mark_groups.shape, jnp.int32),
            pltpu.VMEM(values.shape, f32),
            pltpu.VMEM(field.shape, f32),
            pltpu.VMEM(behind.shape, f32),
            pltpu.VMEM(ahead.shape, f32),
            pltpu.VMEM(ratio.shape, f32),
            pltpu.VMEM((max((owners + 1) * LANES, FILL_ROWS), LANES), f32),
            pltpu.VMEM((FILL_ROWS + TILE, LANES), f32),
            pltpu.VMEM((NV, size + 2 * ROWS + 2 * TILE, LANES), f32),
            pltpu.VMEM((size, LANES), f32),
            pltpu.SemaphoreType.DMA((8,)),
        ],
        compiler_params=pltpu.CompilerParams(vmem_limit_bytes=62 << 20),
        name="fill",
    )(counts, mark_rows, mark_groups, values, field, behind, ahead, ratio)


def on_device(
    field, node_jitter, time_ratio, donor_cell, receptor_offset, receptor_node, point_count
):
    flat_field = field.reshape(NV, CELL_PLANES * ROWS, LANES)
    answers, ahead, behind, mark_rows, mark_groups = donor_values(
        donor_cell[0],
        jnp.moveaxis(receptor_offset[0], 2, 1),
        flat_field,
        node_jitter.reshape(3, CELL_PLANES * ROWS, LANES),
        receptor_node[0],
        point_count,
    )
    out = fill_and_relax(
        point_count,
        mark_rows,
        mark_groups,
        answers,
        flat_field,
        behind,
        ahead,
        time_ratio.reshape(CELL_PLANES * ROWS, LANES),
    )
    return out.reshape(field.shape)


def solution(mesh):
    placed = (
        P(None, ("grid", "sub"), None, None),
        P(None, ("grid", "sub"), None, None),
        P(("grid", "sub"), None, None),
        P(("grid", "sub"), None, None, None),
        P(("grid", "sub"), None, None, None, None),
        P(("grid", "sub"), None, None, None),
        P(("grid", "sub"), None),
    )
    return jax.shard_map(
        on_device,
        mesh=mesh,
        in_specs=placed,
        out_specs=P(None, ("grid", "sub"), None, None),
        check_vma=False,
    )
```

```python
import jax
import jax.numpy as jnp
from jax import lax
from jax.experimental import pallas as pl
from jax.experimental.pallas import tpu as pltpu
from jax.sharding import PartitionSpec as P

LANES = 128
TILE = 8
ROWS = 32
CELL_PLANES = 8
PLANE = ROWS * LANES
NV = 5
UNROLL = 64
HALF_CELLS = CELL_PLANES // 2 * PLANE
FILL_ROWS = (CELL_PLANES - 2) * PLANE // 16


def lerp(low, high, weight):
    return low + weight * (high - low)


def solve_group(places, target):
    size = target[0].shape
    param = [jnp.full(size, 0.5, jnp.float32) for _ in range(3)]
    rise = [
        [[places[m][a][b][1] - places[m][a][b][0] for b in range(2)] for a in range(2)]
        for m in range(3)
    ]
    for _ in range(4):
        u, v, w = param
        misfit, jac = [], []
        for m in range(3):
            edge = [[places[m][a][b][0] + w * rise[m][a][b] for b in range(2)] for a in range(2)]
            across = [edge[a][1] - edge[a][0] for a in range(2)]
            face = [edge[a][0] + v * across[a] for a in range(2)]
            slope0 = face[1] - face[0]
            misfit.append(face[0] + u * slope0 - target[m])
            slope1 = lerp(across[0], across[1], u)
            slope2 = lerp(
                lerp(rise[m][0][0], rise[m][0][1], v), lerp(rise[m][1][0], rise[m][1][1], v), u
            )
            jac.append((slope0, slope1, slope2))
        x, y, z = ([jac[m][d] for m in range(3)] for d in range(3))

        def cross(p, q):
            return [
                p[1] * q[2] - p[2] * q[1],
                p[2] * q[0] - p[0] * q[2],
                p[0] * q[1] - p[1] * q[0],
            ]

        def dot(p, q):
            return p[0] * q[0] + p[1] * q[1] + p[2] * q[2]

        yz, zx, xy = cross(y, z), cross(z, x), cross(x, y)
        inverse = 1.0 / dot(x, yz)
        param = [
            u - dot(misfit, yz) * inverse,
            v - dot(misfit, zx) * inverse,
            w - dot(misfit, xy) * inverse,
        ]
    return param


def donor_kernel(
    cells, offsets, field, jitter, nodes, counts,
    answers, ahead_out, behind_out, mark_rows_out, mark_groups_out,
    ahead, behind, mark_rows, mark_groups, counts_now, cells_in, cells_near, cells_now, offsets_in, field_here, jitter_here, tiles, shifted, table, picked, corners, sent,
    local_sems, halo_send, halo_recv, cell_send, cell_recv, offset_send, offset_recv,
    answer_send, answer_recv,
):
    grids = lax.axis_size("grid")
    subs = lax.axis_size("sub")
    me = lax.axis_index("grid")
    sub = lax.axis_index("sub")
    after, before = lax.rem(me + 1, grids), lax.rem(me + grids - 1, grids)
    sub_after, sub_before = lax.rem(sub + 1, subs), lax.rem(sub + subs - 1, subs)

    barrier = pltpu.get_barrier_semaphore()

    def greet(s, carry):
        pl.semaphore_signal(barrier, inc=1, device_id={"grid": lax.rem(me + s, grids)})
        return carry

    lax.fori_loop(1, grids, greet, 0)
    pl.semaphore_signal(barrier, inc=1, device_id={"sub": sub_after})
    pl.semaphore_signal(barrier, inc=1, device_id={"sub": sub_before})

    loads = [
        pltpu.make_async_copy(field, field_here, local_sems.at[0]),
        pltpu.make_async_copy(jitter, jitter_here, local_sems.at[1]),
    ]
    side_loads = [
        pltpu.make_async_copy(counts.at[0], counts_now, local_sems.at[2]),
        pltpu.make_async_copy(nodes.at[:, 0], mark_rows.at[pl.ds(0, grids)], local_sems.at[3]),
        pltpu.make_async_copy(nodes.at[after, 1], mark_rows.at[grids], local_sems.at[4]),
    ]
    for load in loads + side_loads:
        load.start()
    for load in loads:
        load.wait()

    def put(start, data):
        tiles[pl.ds(start, TILE, stride=TILE), :] = data
        shifted[pl.ds(start, TILE, stride=TILE), :] = pltpu.roll(data, LANES - 1, 1)

    def fill(tile, carry):
        base = pl.multiple_of(tile * TILE, TILE)
        for c in range(NV):
            put(base * TILE + c, field_here[c, pl.ds(base, TILE), :])
        for c in range(3):
            put(base * TILE + NV + c, jitter_here[c, pl.ds(base, TILE), :])
        return carry

    lax.fori_loop(0, CELL_PLANES * ROWS // TILE, fill, 0)
    pl.semaphore_wait(barrier, grids + 1)

    def remote(source, target, send, recv, device):
        return pltpu.make_async_remote_copy(
            src_ref=source, dst_ref=target, send_sem=send, recv_sem=recv, device_id=device
        )

    first, last = pl.ds(0, ROWS), pl.ds((CELL_PLANES - 1) * ROWS, ROWS)
    halos = [
        remote(
            field_here.at[:, first], ahead.at[pl.ds(0, NV)],
            halo_send.at[0], halo_recv.at[0], {"sub": sub_before},
        ),
        remote(
            jitter_here.at[:, first], ahead.at[pl.ds(NV, 3)],
            halo_send.at[1], halo_recv.at[1], {"sub": sub_before},
        ),
        remote(
            field_here.at[:, last], behind, halo_send.at[2], halo_recv.at[2], {"sub": sub_after}
        ),
    ]
    for halo in halos:
        halo.start()

    def cell_copy(peer):
        return remote(
            cells.at[peer, 0], cells_in.at[me], cell_send.at[0], cell_recv.at[0], {"grid": peer}
        )

    def offset_copy(peer):
        return remote(
            offsets.at[peer, :, 0], offsets_in.at[pl.ds(me * TILE, 3)],
            offset_send.at[0], offset_recv.at[0], {"grid": peer},
        )

    def send_cells(s, carry):
        cell_copy(lax.rem(me + s, grids)).start()
        return carry

    def send_offsets(s, carry):
        offset_copy(lax.rem(me + s, grids)).start()
        return carry

    lax.fori_loop(1, grids, send_cells, 0)
    more_cells = remote(
        cells.at[after, 1], cells_in.at[grids], cell_send.at[1], cell_recv.at[1], {"grid": after}
    )
    more_cells.start()
    own_cells = pltpu.make_async_copy(cells.at[me, 0], cells_in.at[me], local_sems.at[0])
    own_cells.start()
    lax.fori_loop(1, grids, send_offsets, 0)
    more_offsets = remote(
        offsets.at[after, :, 1], offsets_in.at[pl.ds(grids * TILE, 3)],
        offset_send.at[1], offset_recv.at[1], {"grid": after},
    )
    more_offsets.start()
    own_offsets = pltpu.make_async_copy(
        offsets.at[me, :, 0], offsets_in.at[pl.ds(me * TILE, 3)], local_sems.at[1]
    )
    own_offsets.start()

    for load in side_loads:
        load.wait()
    slot = lax.broadcasted_iota(jnp.int32, (1, LANES), 1)

    def mark(o, live):
        node = mark_rows[pl.ds(o, 1), :]
        place = (((node >> 11) - 2) << 7) + (node & (LANES - 1))
        mark_rows[pl.ds(o, 1), :] = jnp.where(slot < live, place, FILL_ROWS)
        mark_groups[pl.ds(o, 1), :] = (node >> 7) & 15

    def mark_step(o, carry):
        mark(o, counts_now[o])
        return carry

    lax.fori_loop(0, grids, mark_step, 0)
    mark(grids, counts_now[after] - LANES)
    stores = [
        pltpu.make_async_copy(mark_rows, mark_rows_out, local_sems.at[3]),
        pltpu.make_async_copy(mark_groups, mark_groups_out, local_sems.at[4]),
        pltpu.make_async_copy(ahead, ahead_out, local_sems.at[5]),
        pltpu.make_async_copy(behind, behind_out, local_sems.at[6]),
    ]
    stores[0].start()
    stores[1].start()

    def build_some(q, carry):
        for step in range(4):
            row = q * 4 + step
            parts = []
            for half in range(2):
                for a in (0, 1, ROWS, ROWS + 1):
                    start = (row + half * (CELL_PLANES // 2) * ROWS + a) * TILE
                    start = pl.multiple_of(start, TILE)
                    parts.append(tiles[pl.ds(start, TILE), :])
                    parts.append(shifted[pl.ds(start, TILE), :])
            table[pl.ds(pl.multiple_of(row * LANES, LANES), LANES), :] = jnp.concatenate(
                parts, 0
            ).T
        return carry

    quarter = ROWS // 4
    lax.fori_loop(0, 3 * quarter, build_some, 0)
    for halo in halos:
        halo.wait_recv()
    stores[2].start()
    stores[3].start()
    for tile in range(ROWS // TILE):
        for c in range(8):
            put(
                (CELL_PLANES * ROWS + tile * TILE) * TILE + c,
                ahead[c, pl.ds(tile * TILE, TILE), :],
            )

    def drain(buffer, sem):
        pltpu.make_async_copy(buffer, buffer, sem).wait()

    drain(cells_in.at[pl.ds(0, grids - 1)], cell_recv.at[0])
    own_cells.wait()
    more_cells.wait_recv()
    cells_near[...] = cells_in[...] & (HALF_CELLS - 1)
    load_cells = pltpu.make_async_copy(cells_near, cells_now, local_sems.at[0])
    load_cells.start()
    lax.fori_loop(3 * quarter, 4 * quarter, build_some, 0)
    load_cells.wait()
    drain(picked.at[pl.ds(0, 3 * (grids - 1))], offset_recv.at[0])
    own_offsets.wait()
    more_offsets.wait_recv()

    def pick(block, count):
        def one(r, carry):
            to = pl.multiple_of(r * LANES, LANES)
            for t in range(LANES):
                picked[pl.ds(to + t, 1), :] = table[pl.ds(cells_now[block + r, t], 1), :]
            return carry

        lax.fori_loop(0, count, one, 0)

    def turn(block, r):
        values = picked[r * LANES : (r + 1) * LANES, :].T
        far = cells_in[pl.ds(block + r, 1), :] >= HALF_CELLS
        for q in range(8):
            corners[q, r * TILE : (r + 1) * TILE, :] = jnp.where(
                far, values[64 + 8 * q : 72 + 8 * q], values[8 * q : 8 * q + 8]
            )

    def solve(block):
        target = [
            offsets_in[pl.ds(block * TILE + m, TILE, stride=TILE), :] for m in range(3)
        ]
        places = [
            [
                [
                    [
                        corners[4 * a + 2 * b + d, pl.ds(NV + m, TILE, stride=TILE), :]
                        + float((a, b, d)[m])
                        for d in range(2)
                    ]
                    for b in range(2)
                ]
                for a in range(2)
            ]
            for m in range(3)
        ]
        u, v, w = solve_group(places, target)
        for c in range(NV):
            node = [corners[q, pl.ds(c, TILE, stride=TILE), :] for q in range(8)]
            edge = [lerp(node[2 * e], node[2 * e + 1], w) for e in range(4)]
            value = lerp(lerp(edge[0], edge[1], v), lerp(edge[2], edge[3], v), u)
            sent[pl.ds(block * TILE + c, TILE, stride=TILE), :] = value

    own_answer = pltpu.make_async_copy(
        sent.at[pl.ds(me * TILE, NV)], answers.at[pl.ds(me * TILE, NV)], local_sems.at[0]
    )

    def group(g, carry):
        block = pl.multiple_of(lax.rem(me // TILE + g, grids // TILE) * TILE, TILE)
        pick(block, TILE)
        for r in range(TILE):
            turn(block, r)
        solve(block)

        def answer(r, carry):
            peer = block + r

            @pl.when(peer != me)
            def _():
                remote(
                    sent.at[pl.ds(peer * TILE, NV)], answers.at[pl.ds(me * TILE, NV)],
                    answer_send.at[0], answer_recv.at[0], {"grid": peer},
                ).start()

            @pl.when(peer == me)
            def _():
                own_answer.start()

            return carry

        lax.fori_loop(0, TILE, answer, 0)
        return carry

    lax.fori_loop(0, grids // TILE, group, 0)
    pick(grids, 1)
    turn(grids, 0)
    solve(grids)
    more_answers = remote(
        sent.at[pl.ds(grids * TILE, NV)], answers.at[pl.ds(grids * TILE, NV)],
        answer_send.at[1], answer_recv.at[1], {"grid": before},
    )
    more_answers.start()

    drain(picked.at[pl.ds(0, NV * (grids - 1))], answer_recv.at[0])
    own_answer.wait()
    more_answers.wait()
    drain(picked.at[pl.ds(0, NV * (grids - 1))], answer_send.at[0])
    drain(cells_in.at[pl.ds(0, grids - 1)], cell_send.at[0])
    drain(picked.at[pl.ds(0, 3 * (grids - 1))], offset_send.at[0])
    more_cells.wait_send()
    more_offsets.wait_send()
    for halo in halos:
        halo.wait_send()
    for store in stores:
        store.wait()


def donor_values(cells, offsets, field, jitter, nodes, counts):
    grids = cells.shape[0]
    padded = grids + TILE
    node_rows = (CELL_PLANES + 1) * ROWS
    hbm = pl.BlockSpec(memory_space=pltpu.HBM)
    f32 = jnp.float32
    return pl.pallas_call(
        donor_kernel,
        out_shape=(
            jax.ShapeDtypeStruct(((grids + 1) * TILE, LANES), f32),
            jax.ShapeDtypeStruct((8, ROWS, LANES), f32),
            jax.ShapeDtypeStruct((NV, ROWS, LANES), f32),
            jax.ShapeDtypeStruct((padded, LANES), jnp.int32),
            jax.ShapeDtypeStruct((padded, LANES), jnp.int32),
        ),
        in_specs=[hbm] * 6,
        out_specs=(hbm,) * 5,
        scratch_shapes=[
            pltpu.VMEM((8, ROWS, LANES), f32),
            pltpu.VMEM((NV, ROWS, LANES), f32),
            pltpu.VMEM((padded, LANES), jnp.int32),
            pltpu.VMEM((padded, LANES), jnp.int32),
            pltpu.SMEM((grids,), jnp.int32),
            pltpu.VMEM((padded, LANES), jnp.int32),
            pltpu.VMEM((padded, LANES), jnp.int32),
            pltpu.SMEM((padded, LANES), jnp.int32),
            pltpu.VMEM((padded * TILE, LANES), f32),
            pltpu.VMEM(field.shape, f32),
            pltpu.VMEM(jitter.shape, f32),
            pltpu.VMEM((node_rows * TILE + 2 * TILE, LANES), f32),
            pltpu.VMEM((node_rows * TILE + 2 * TILE, LANES), f32),
            pltpu.VMEM((HALF_CELLS, LANES), f32),
            pltpu.VMEM((TILE * LANES, LANES), f32),
            pltpu.VMEM((8, TILE * TILE, LANES), f32),
            pltpu.VMEM((padded * TILE, LANES), f32),
        ]
        + [pltpu.SemaphoreType.DMA((n,)) for n in (7, 3, 3, 2, 2, 2, 2, 2, 2)],
        compiler_params=pltpu.CompilerParams(
            collective_id=0, has_side_effects=True, vmem_limit_bytes=60 << 20
        ),
        name="donor",
    )(cells, offsets, field, jitter, nodes, counts)


def fill_kernel(
    counts_in, mark_rows_in, mark_groups_in, values_in, field_in, behind_in, ahead_in, ratio_in, out,
    counts, mark_rows, mark_groups, values, field, behind, ahead, ratio,
    turned, rows, filled, fringes, result, sems, out_sem,
):
    owners = counts.shape[0]
    loads = [
        pltpu.make_async_copy(source, target, sems.at[n])
        for n, (source, target) in enumerate(
            (
                (values_in, values),
                (mark_rows_in, mark_rows),
                (mark_groups_in, mark_groups),
                (counts_in.at[0], counts),
                (field_in, field),
                (behind_in, behind),
                (ahead_in, ahead),
                (ratio_in, ratio),
            )
        )
    ]
    for load in loads:
        load.start()
    size = CELL_PLANES * ROWS
    lane = lax.broadcasted_iota(jnp.int32, (TILE, LANES), 1)
    level = lax.broadcasted_iota(jnp.int32, (TILE, LANES), 0)

    def clear(q, carry):
        rows[pl.ds(pl.multiple_of(q * LANES, LANES), LANES), :] = jnp.zeros(
            (LANES, LANES), jnp.float32
        )
        return carry

    lax.fori_loop(0, FILL_ROWS // LANES, clear, 0)
    loads[0].wait()
    loads[2].wait()

    def spread(o):
        block = values[pl.ds(pl.multiple_of(o * TILE, TILE), TILE), :]
        block = jnp.where(level < NV, block, 1.0)
        choice = jnp.broadcast_to(mark_groups[pl.ds(o, 1), :], (TILE, LANES))
        parts = [jnp.where(choice == g, block, jnp.inf) for g in range(16)]
        start = pl.multiple_of(o * LANES, LANES)
        turned[pl.ds(start, LANES), :] = jnp.concatenate(parts, 0).T

    def spread_some(g, carry):
        for step in range(4):
            spread(g * 4 + step)
        return carry

    lax.fori_loop(0, owners // 4, spread_some, 0)
    spread(owners)

    loads[1].wait()
    loads[3].wait()

    def scatter(o, live):
        first = pl.multiple_of(o * LANES, LANES)
        for start in range(0, LANES, UNROLL):

            @pl.when(live > start)
            def _():
                for t in range(start, start + UNROLL):
                    row = turned[pl.ds(first + t, 1), :]
                    pltpu.store(
                        rows.at[pl.ds(mark_rows[o, t], 1), :], row, mask=row < jnp.inf
                    )

    def scatter_step(o, carry):
        scatter(o, jnp.minimum(counts[o], LANES))
        return carry

    lax.fori_loop(0, owners, scatter_step, 0)
    scatter(owners, LANES)

    def back(q):
        start = pl.multiple_of(q * LANES, LANES)
        turned[pl.ds(start, LANES), :] = rows[pl.ds(start, LANES), :].T

    def back_some(g, carry):
        for step in range(4):
            back(g * 4 + step)
        return carry

    lax.fori_loop(0, FILL_ROWS // LANES // 4, back_some, 0)

    for load in loads[4:]:
        load.wait()

    for c in range(NV):
        filled[c, 0:TILE, :] = jnp.zeros((TILE, LANES), jnp.float32)
        for plane, data in (
            (0, behind[c]),
            (1, field[c, 0:ROWS, :]),
            (CELL_PLANES, field[c, size - ROWS : size, :]),
            (CELL_PLANES + 1, ahead[c]),
        ):
            filled[c, TILE + plane * ROWS : TILE + (plane + 1) * ROWS, :] = data
    for edge in (0, size - ROWS):
        fringes[edge : edge + ROWS, :] = jnp.zeros((ROWS, LANES), jnp.float32)

    def merge(tile, carry):
        base = pl.multiple_of(tile * TILE, TILE)
        inner = pl.multiple_of(base + ROWS, TILE)
        flag = turned[pl.ds(base * TILE + NV, TILE, stride=TILE), :]
        fringes[pl.ds(inner, TILE), :] = flag
        for c in range(NV):
            filled[c, pl.ds(pl.multiple_of(inner + ROWS + TILE, TILE), TILE), :] = jnp.where(
                flag > 0.5,
                turned[pl.ds(base * TILE + c, TILE, stride=TILE), :],
                field[c, pl.ds(inner, TILE), :],
            )
        return carry

    lax.fori_loop(0, (CELL_PLANES - 2) * ROWS // TILE, merge, 0)

    def relax(i, carry):
        for part in range(ROWS // TILE):
            base = pl.multiple_of(i * ROWS + part * TILE, TILE)
            here = base + ROWS + TILE
            rate = ratio[pl.ds(base, TILE), :]
            scale = 1.0 / (1.0 + 6.0 * rate)
            fringe = fringes[pl.ds(base, TILE), :] > 0.5
            for c in range(NV):
                mid = filled[c, pl.ds(pl.multiple_of(here, TILE), TILE), :]
                up = filled[c, pl.ds(here + 1, TILE), :]
                down = filled[c, pl.ds(here - 1, TILE), :]
                if part == 0:
                    down = jnp.where(level == 0, 0.0, down)
                if part == ROWS // TILE - 1:
                    up = jnp.where(level == TILE - 1, 0.0, up)
                left = jnp.where(lane == 0, 0.0, pltpu.roll(mid, 1, 1))
                right = jnp.where(lane == LANES - 1, 0.0, pltpu.roll(mid, LANES - 1, 1))
                total = (
                    filled[c, pl.ds(pl.multiple_of(here + ROWS, TILE), TILE), :]
                    + filled[c, pl.ds(pl.multiple_of(here - ROWS, TILE), TILE), :]
                    + up
                    + down
                    + left
                    + right
                )
                result[c, pl.ds(base, TILE), :] = jnp.where(
                    fringe, mid, (mid + rate * total) * scale
                )
        plane_out(i).start()
        return carry

    def plane_out(i):
        plane = pl.ds(pl.multiple_of(i * ROWS, ROWS), ROWS)
        return pltpu.make_async_copy(result.at[:, plane], out.at[:, plane], out_sem.at[i])

    lax.fori_loop(0, CELL_PLANES, relax, 0)
    for i in range(CELL_PLANES):
        plane_out(i).wait()


def fill_and_relax(counts, mark_rows, mark_groups, values, field, behind, ahead, ratio):
    owners = counts.shape[1]
    size = CELL_PLANES * ROWS
    hbm = pl.BlockSpec(memory_space=pltpu.HBM)
    f32 = jnp.float32
    return pl.pallas_call(
        fill_kernel,
        out_shape=jax.ShapeDtypeStruct(field.shape, f32),
        in_specs=[hbm] * 8,
        out_specs=hbm,
        scratch_shapes=[
            pltpu.SMEM((owners,), jnp.int32),
            pltpu.SMEM(mark_rows.shape, jnp.int32),
            pltpu.VMEM(mark_groups.shape, jnp.int32),
            pltpu.VMEM(values.shape, f32),
            pltpu.VMEM(field.shape, f32),
            pltpu.VMEM(behind.shape, f32),
            pltpu.VMEM(ahead.shape, f32),
            pltpu.VMEM(ratio.shape, f32),
            pltpu.VMEM((max((owners + 1) * LANES, FILL_ROWS), LANES), f32),
            pltpu.VMEM((FILL_ROWS + TILE, LANES), f32),
            pltpu.VMEM((NV, size + 2 * ROWS + 2 * TILE, LANES), f32),
            pltpu.VMEM((size, LANES), f32),
            pltpu.VMEM(field.shape, f32),
            pltpu.SemaphoreType.DMA((8,)),
            pltpu.SemaphoreType.DMA((CELL_PLANES,)),
        ],
        compiler_params=pltpu.CompilerParams(vmem_limit_bytes=62 << 20),
        name="fill",
    )(counts, mark_rows, mark_groups, values, field, behind, ahead, ratio)


def on_device(
    field, node_jitter, time_ratio, donor_cell, receptor_offset, receptor_node, point_count
):
    flat_field = field.reshape(NV, CELL_PLANES * ROWS, LANES)
    answers, ahead, behind, mark_rows, mark_groups = donor_values(
        donor_cell[0],
        jnp.moveaxis(receptor_offset[0], 2, 1),
        flat_field,
        node_jitter.reshape(3, CELL_PLANES * ROWS, LANES),
        receptor_node[0],
        point_count,
    )
    out = fill_and_relax(
        point_count,
        mark_rows,
        mark_groups,
        answers,
        flat_field,
        behind,
        ahead,
        time_ratio.reshape(CELL_PLANES * ROWS, LANES),
    )
    return out.reshape(field.shape)


def solution(mesh):
    placed = (
        P(None, ("grid", "sub"), None, None),
        P(None, ("grid", "sub"), None, None),
        P(("grid", "sub"), None, None),
        P(("grid", "sub"), None, None, None),
        P(("grid", "sub"), None, None, None, None),
        P(("grid", "sub"), None, None, None),
        P(("grid", "sub"), None),
    )
    return jax.shard_map(
        on_device,
        mesh=mesh,
        in_specs=placed,
        out_specs=P(None, ("grid", "sub"), None, None),
        check_vma=False,
    )
```

```python
import jax
import jax.numpy as jnp
from jax import lax
from jax.experimental import pallas as pl
from jax.experimental.pallas import tpu as pltpu
from jax.sharding import PartitionSpec as P

LANES = 128
TILE = 8
ROWS = 32
CELL_PLANES = 8
PLANE = ROWS * LANES
NV = 5
UNROLL = 64
HALF_CELLS = CELL_PLANES // 2 * PLANE
FILL_ROWS = (CELL_PLANES - 2) * PLANE // 16


def lerp(low, high, weight):
    return low + weight * (high - low)


def solve_group(places, target):
    size = target[0].shape
    param = [jnp.full(size, 0.5, jnp.float32) for _ in range(3)]
    rise = [
        [[places[m][a][b][1] - places[m][a][b][0] for b in range(2)] for a in range(2)]
        for m in range(3)
    ]
    for _ in range(4):
        u, v, w = param
        misfit, jac = [], []
        for m in range(3):
            edge = [[places[m][a][b][0] + w * rise[m][a][b] for b in range(2)] for a in range(2)]
            across = [edge[a][1] - edge[a][0] for a in range(2)]
            face = [edge[a][0] + v * across[a] for a in range(2)]
            slope0 = face[1] - face[0]
            misfit.append(face[0] + u * slope0 - target[m])
            slope1 = lerp(across[0], across[1], u)
            slope2 = lerp(
                lerp(rise[m][0][0], rise[m][0][1], v), lerp(rise[m][1][0], rise[m][1][1], v), u
            )
            jac.append((slope0, slope1, slope2))
        x, y, z = ([jac[m][d] for m in range(3)] for d in range(3))

        def cross(p, q):
            return [
                p[1] * q[2] - p[2] * q[1],
                p[2] * q[0] - p[0] * q[2],
                p[0] * q[1] - p[1] * q[0],
            ]

        def dot(p, q):
            return p[0] * q[0] + p[1] * q[1] + p[2] * q[2]

        yz, zx, xy = cross(y, z), cross(z, x), cross(x, y)
        inverse = 1.0 / dot(x, yz)
        param = [
            u - dot(misfit, yz) * inverse,
            v - dot(misfit, zx) * inverse,
            w - dot(misfit, xy) * inverse,
        ]
    return param


def wrap(index, count):
    return index & (count - 1) if count & (count - 1) == 0 else lax.rem(index, count)


def donor_kernel(
    cells_hbm, offsets_hbm, field, jitter, nodes, counts,
    answers, ahead_out, behind_out, mark_rows_out, mark_groups_out,
    cells, offsets, ahead, behind, mark_rows, mark_groups, counts_now, cells_in, cells_near, cells_now, offsets_in, field_here, jitter_here, tiles, shifted, table, picked, corners, sent,
    local_sems, halo_send, halo_recv, cell_send, cell_recv, offset_send, offset_recv,
    answer_send, answer_recv,
):
    grids = lax.axis_size("grid")
    subs = lax.axis_size("sub")
    me = lax.axis_index("grid")
    sub = lax.axis_index("sub")
    after, before = wrap(me + 1, grids), wrap(me + grids - 1, grids)
    sub_after, sub_before = wrap(sub + 1, subs), wrap(sub + subs - 1, subs)

    barrier = pltpu.get_barrier_semaphore()

    def greet(s, carry):
        pl.semaphore_signal(barrier, inc=1, device_id={"grid": wrap(me + s, grids)})
        return carry

    lax.fori_loop(1, grids, greet, 0, unroll=7)
    pl.semaphore_signal(barrier, inc=1, device_id={"sub": sub_after})
    pl.semaphore_signal(barrier, inc=1, device_id={"sub": sub_before})

    loads = [
        pltpu.make_async_copy(field, field_here, local_sems.at[0]),
        pltpu.make_async_copy(jitter, jitter_here, local_sems.at[1]),
        pltpu.make_async_copy(cells_hbm, cells, local_sems.at[5]),
        pltpu.make_async_copy(offsets_hbm, offsets, local_sems.at[6]),
    ]
    side_loads = [
        pltpu.make_async_copy(counts.at[0], counts_now, local_sems.at[2]),
        pltpu.make_async_copy(nodes.at[:, 0], mark_rows.at[pl.ds(0, grids)], local_sems.at[3]),
        pltpu.make_async_copy(nodes.at[after, 1], mark_rows.at[grids], local_sems.at[4]),
    ]
    for load in loads + side_loads:
        load.start()
    for load in loads:
        load.wait()

    def put(start, data):
        tiles[pl.ds(start, TILE, stride=TILE), :] = data
        shifted[pl.ds(start, TILE, stride=TILE), :] = pltpu.roll(data, LANES - 1, 1)

    def fill(tile, carry):
        base = pl.multiple_of(tile * TILE, TILE)
        for c in range(NV):
            put(base * TILE + c, field_here[c, pl.ds(base, TILE), :])
        for c in range(3):
            put(base * TILE + NV + c, jitter_here[c, pl.ds(base, TILE), :])
        return carry

    lax.fori_loop(0, CELL_PLANES * ROWS // TILE, fill, 0)
    pl.semaphore_wait(barrier, grids + 1)

    def remote(source, target, send, recv, device):
        return pltpu.make_async_remote_copy(
            src_ref=source, dst_ref=target, send_sem=send, recv_sem=recv, device_id=device
        )

    first, last = pl.ds(0, ROWS), pl.ds((CELL_PLANES - 1) * ROWS, ROWS)
    halos = [
        remote(
            field_here.at[:, first], ahead.at[pl.ds(0, NV)],
            halo_send.at[0], halo_recv.at[0], {"sub": sub_before},
        ),
        remote(
            jitter_here.at[:, first], ahead.at[pl.ds(NV, 3)],
            halo_send.at[1], halo_recv.at[1], {"sub": sub_before},
        ),
        remote(
            field_here.at[:, last], behind, halo_send.at[2], halo_recv.at[2], {"sub": sub_after}
        ),
    ]
    for halo in halos:
        halo.start()

    def cell_copy(peer):
        return remote(
            cells.at[peer, 0], cells_in.at[me], cell_send.at[0], cell_recv.at[0], {"grid": peer}
        )

    def offset_copy(peer):
        return remote(
            offsets.at[peer, :, 0], offsets_in.at[pl.ds(me * TILE, 3)],
            offset_send.at[0], offset_recv.at[0], {"grid": peer},
        )

    def send_cells(s, carry):
        cell_copy(wrap(me + s, grids)).start()
        return carry

    def send_offsets(s, carry):
        offset_copy(wrap(me + s, grids)).start()
        return carry

    lax.fori_loop(1, grids, send_cells, 0, unroll=7)
    more_cells = remote(
        cells.at[after, 1], cells_in.at[grids], cell_send.at[1], cell_recv.at[1], {"grid": after}
    )
    more_cells.start()
    own_cells = pltpu.make_async_copy(cells.at[me, 0], cells_in.at[me], local_sems.at[0])
    own_cells.start()
    lax.fori_loop(1, grids, send_offsets, 0, unroll=7)
    more_offsets = remote(
        offsets.at[after, :, 1], offsets_in.at[pl.ds(grids * TILE, 3)],
        offset_send.at[1], offset_recv.at[1], {"grid": after},
    )
    more_offsets.start()
    own_offsets = pltpu.make_async_copy(
        offsets.at[me, :, 0], offsets_in.at[pl.ds(me * TILE, 3)], local_sems.at[1]
    )
    own_offsets.start()

    for load in side_loads:
        load.wait()
    slot = lax.broadcasted_iota(jnp.int32, (1, LANES), 1)

    def mark(o, live):
        node = mark_rows[pl.ds(o, 1), :]
        place = (((node >> 11) - 2) << 7) + (node & (LANES - 1))
        mark_rows[pl.ds(o, 1), :] = jnp.where(slot < live, place, FILL_ROWS)
        mark_groups[pl.ds(o, 1), :] = (node >> 7) & 15

    def mark_step(o, carry):
        mark(o, counts_now[o])
        return carry

    lax.fori_loop(0, grids, mark_step, 0)
    mark(grids, counts_now[after] - LANES)
    stores = [
        pltpu.make_async_copy(mark_rows, mark_rows_out, local_sems.at[3]),
        pltpu.make_async_copy(mark_groups, mark_groups_out, local_sems.at[4]),
        pltpu.make_async_copy(ahead, ahead_out, local_sems.at[5]),
        pltpu.make_async_copy(behind, behind_out, local_sems.at[6]),
    ]
    stores[0].start()
    stores[1].start()

    def build_some(q, carry):
        for step in range(4):
            row = q * 4 + step
            parts = []
            for half in range(2):
                for a in (0, 1, ROWS, ROWS + 1):
                    start = (row + half * (CELL_PLANES // 2) * ROWS + a) * TILE
                    start = pl.multiple_of(start, TILE)
                    parts.append(tiles[pl.ds(start, TILE), :])
                    parts.append(shifted[pl.ds(start, TILE), :])
            table[pl.ds(pl.multiple_of(row * LANES, LANES), LANES), :] = jnp.concatenate(
                parts, 0
            ).T
        return carry

    quarter = ROWS // 4
    lax.fori_loop(0, 3 * quarter, build_some, 0)
    for halo in halos:
        halo.wait_recv()
    stores[2].start()
    stores[3].start()
    for tile in range(ROWS // TILE):
        for c in range(8):
            put(
                (CELL_PLANES * ROWS + tile * TILE) * TILE + c,
                ahead[c, pl.ds(tile * TILE, TILE), :],
            )

    def drain(buffer, sem):
        pltpu.make_async_copy(buffer, buffer, sem).wait()

    drain(cells_in.at[pl.ds(0, grids - 1)], cell_recv.at[0])
    own_cells.wait()
    more_cells.wait_recv()
    cells_near[...] = cells_in[...] & (HALF_CELLS - 1)
    load_cells = pltpu.make_async_copy(cells_near, cells_now, local_sems.at[0])
    load_cells.start()
    lax.fori_loop(3 * quarter, 4 * quarter, build_some, 0)
    load_cells.wait()

    def pick(block, count):
        def one(r, carry):
            to = pl.multiple_of(r * LANES, LANES)
            for t in range(LANES):
                picked[pl.ds(to + t, 1), :] = table[pl.ds(cells_now[block + r, t], 1), :]
            return carry

        lax.fori_loop(0, count, one, 0)

    def turn(block, r):
        values = picked[r * LANES : (r + 1) * LANES, :].T
        far = cells_in[pl.ds(block + r, 1), :] >= HALF_CELLS
        for q in range(8):
            corners[q, r * TILE : (r + 1) * TILE, :] = jnp.where(
                far, values[64 + 8 * q : 72 + 8 * q], values[8 * q : 8 * q + 8]
            )

    def solve(block):
        target = [
            offsets_in[pl.ds(block * TILE + m, TILE, stride=TILE), :] for m in range(3)
        ]
        places = [
            [
                [
                    [
                        corners[4 * a + 2 * b + d, pl.ds(NV + m, TILE, stride=TILE), :]
                        + float((a, b, d)[m])
                        for d in range(2)
                    ]
                    for b in range(2)
                ]
                for a in range(2)
            ]
            for m in range(3)
        ]
        u, v, w = solve_group(places, target)
        for c in range(NV):
            node = [corners[q, pl.ds(c, TILE, stride=TILE), :] for q in range(8)]
            edge = [lerp(node[2 * e], node[2 * e + 1], w) for e in range(4)]
            value = lerp(lerp(edge[0], edge[1], v), lerp(edge[2], edge[3], v), u)
            sent[pl.ds(block * TILE + c, TILE, stride=TILE), :] = value

    own_answer = pltpu.make_async_copy(
        sent.at[pl.ds(me * TILE, NV)], answers.at[pl.ds(me * TILE, NV)], local_sems.at[0]
    )

    def group(g, carry):
        block = pl.multiple_of(wrap((me >> 3) + g, grids // TILE) * TILE, TILE)
        pick(block, TILE)
        for r in range(TILE):
            turn(block, r)
        @pl.when(g == 0)
        def _():
            drain(picked.at[pl.ds(0, 3 * (grids - 1))], offset_recv.at[0])
            own_offsets.wait()
            more_offsets.wait_recv()

        solve(block)

        for r in range(TILE):
            peer = block + r

            @pl.when(peer != me)
            def _():
                remote(
                    sent.at[pl.ds(peer * TILE, NV)], answers.at[pl.ds(me * TILE, NV)],
                    answer_send.at[0], answer_recv.at[0], {"grid": peer},
                ).start()

            @pl.when(peer == me)
            def _():
                own_answer.start()

        return carry

    lax.fori_loop(0, grids // TILE, group, 0)
    pick(grids, 1)
    turn(grids, 0)
    solve(grids)
    more_answers = remote(
        sent.at[pl.ds(grids * TILE, NV)], answers.at[pl.ds(grids * TILE, NV)],
        answer_send.at[1], answer_recv.at[1], {"grid": before},
    )
    more_answers.start()

    drain(picked.at[pl.ds(0, NV * (grids - 1))], answer_recv.at[0])
    own_answer.wait()
    more_answers.wait()
    drain(picked.at[pl.ds(0, NV * (grids - 1))], answer_send.at[0])
    drain(cells_in.at[pl.ds(0, grids - 1)], cell_send.at[0])
    drain(picked.at[pl.ds(0, 3 * (grids - 1))], offset_send.at[0])
    more_cells.wait_send()
    more_offsets.wait_send()
    for halo in halos:
        halo.wait_send()
    for store in stores:
        store.wait()


def donor_values(cells, offsets, field, jitter, nodes, counts):
    grids = cells.shape[0]
    padded = grids + TILE
    node_rows = (CELL_PLANES + 1) * ROWS
    hbm = pl.BlockSpec(memory_space=pltpu.HBM)
    f32 = jnp.float32
    return pl.pallas_call(
        donor_kernel,
        out_shape=(
            jax.ShapeDtypeStruct(((grids + 1) * TILE, LANES), f32),
            jax.ShapeDtypeStruct((8, ROWS, LANES), f32),
            jax.ShapeDtypeStruct((NV, ROWS, LANES), f32),
            jax.ShapeDtypeStruct((padded, LANES), jnp.int32),
            jax.ShapeDtypeStruct((padded, LANES), jnp.int32),
        ),
        in_specs=[hbm] * 6,
        out_specs=(hbm,) * 5,
        scratch_shapes=[
            pltpu.VMEM(cells.shape, jnp.int32),
            pltpu.VMEM(offsets.shape, f32),
            pltpu.VMEM((8, ROWS, LANES), f32),
            pltpu.VMEM((NV, ROWS, LANES), f32),
            pltpu.VMEM((padded, LANES), jnp.int32),
            pltpu.VMEM((padded, LANES), jnp.int32),
            pltpu.SMEM((grids,), jnp.int32),
            pltpu.VMEM((padded, LANES), jnp.int32),
            pltpu.VMEM((padded, LANES), jnp.int32),
            pltpu.SMEM((padded, LANES), jnp.int32),
            pltpu.VMEM((padded * TILE, LANES), f32),
            pltpu.VMEM(field.shape, f32),
            pltpu.VMEM(jitter.shape, f32),
            pltpu.VMEM((node_rows * TILE + 2 * TILE, LANES), f32),
            pltpu.VMEM((node_rows * TILE + 2 * TILE, LANES), f32),
            pltpu.VMEM((HALF_CELLS, LANES), f32),
            pltpu.VMEM((TILE * LANES, LANES), f32),
            pltpu.VMEM((8, TILE * TILE, LANES), f32),
            pltpu.VMEM((padded * TILE, LANES), f32),
        ]
        + [pltpu.SemaphoreType.DMA((n,)) for n in (7, 3, 3, 2, 2, 2, 2, 2, 2)],
        compiler_params=pltpu.CompilerParams(
            collective_id=0, has_side_effects=True, vmem_limit_bytes=60 << 20
        ),
        name="donor",
    )(cells, offsets, field, jitter, nodes, counts)


def fill_kernel(
    counts_in, mark_rows_in, mark_groups_in, values_in, field_in, behind_in, ahead_in, ratio_in, out,
    counts, mark_rows, mark_groups, values, field, behind, ahead, ratio,
    turned, rows, filled, fringes, result, sems, out_sem,
):
    owners = counts.shape[0]
    loads = [
        pltpu.make_async_copy(source, target, sems.at[n])
        for n, (source, target) in enumerate(
            (
                (values_in, values),
                (mark_rows_in, mark_rows),
                (mark_groups_in, mark_groups),
                (counts_in.at[0], counts),
                (field_in, field),
                (behind_in, behind),
                (ahead_in, ahead),
                (ratio_in, ratio),
            )
        )
    ]
    for load in loads:
        load.start()
    size = CELL_PLANES * ROWS
    lane = lax.broadcasted_iota(jnp.int32, (TILE, LANES), 1)
    level = lax.broadcasted_iota(jnp.int32, (TILE, LANES), 0)

    def clear(q, carry):
        rows[pl.ds(pl.multiple_of(q * LANES, LANES), LANES), :] = jnp.zeros(
            (LANES, LANES), jnp.float32
        )
        return carry

    lax.fori_loop(0, FILL_ROWS // LANES, clear, 0)
    loads[0].wait()
    loads[2].wait()

    def spread(o):
        block = values[pl.ds(pl.multiple_of(o * TILE, TILE), TILE), :]
        block = jnp.where(level < NV, block, 1.0)
        choice = jnp.broadcast_to(mark_groups[pl.ds(o, 1), :], (TILE, LANES))
        parts = [jnp.where(choice == g, block, jnp.inf) for g in range(16)]
        start = pl.multiple_of(o * LANES, LANES)
        turned[pl.ds(start, LANES), :] = jnp.concatenate(parts, 0).T

    def spread_some(g, carry):
        for step in range(8):
            spread(g * 8 + step)
        return carry

    lax.fori_loop(0, owners // 8, spread_some, 0)
    spread(owners)

    loads[1].wait()
    loads[3].wait()

    def scatter(o, live):
        first = pl.multiple_of(o * LANES, LANES)
        for start in range(0, LANES, UNROLL):

            @pl.when(live > start)
            def _():
                for t in range(start, start + UNROLL):
                    row = turned[pl.ds(first + t, 1), :]
                    pltpu.store(
                        rows.at[pl.ds(mark_rows[o, t], 1), :], row, mask=row < jnp.inf
                    )

    def scatter_step(o, carry):
        scatter(o, jnp.minimum(counts[o], LANES))
        return carry

    lax.fori_loop(0, owners, scatter_step, 0)
    scatter(owners, LANES)

    def back(q):
        start = pl.multiple_of(q * LANES, LANES)
        turned[pl.ds(start, LANES), :] = rows[pl.ds(start, LANES), :].T

    def back_some(g, carry):
        for step in range(4):
            back(g * 4 + step)
        return carry

    lax.fori_loop(0, FILL_ROWS // LANES // 4, back_some, 0)

    for load in loads[4:]:
        load.wait()

    for c in range(NV):
        filled[c, 0:TILE, :] = jnp.zeros((TILE, LANES), jnp.float32)
        for plane, data in (
            (0, behind[c]),
            (1, field[c, 0:ROWS, :]),
            (CELL_PLANES, field[c, size - ROWS : size, :]),
            (CELL_PLANES + 1, ahead[c]),
        ):
            filled[c, TILE + plane * ROWS : TILE + (plane + 1) * ROWS, :] = data
    for edge in (0, size - ROWS):
        fringes[edge : edge + ROWS, :] = jnp.zeros((ROWS, LANES), jnp.float32)

    def merge(tile, carry):
        base = pl.multiple_of(tile * TILE, TILE)
        inner = pl.multiple_of(base + ROWS, TILE)
        flag = turned[pl.ds(base * TILE + NV, TILE, stride=TILE), :]
        fringes[pl.ds(inner, TILE), :] = flag
        for c in range(NV):
            filled[c, pl.ds(pl.multiple_of(inner + ROWS + TILE, TILE), TILE), :] = jnp.where(
                flag > 0.5,
                turned[pl.ds(base * TILE + c, TILE, stride=TILE), :],
                field[c, pl.ds(inner, TILE), :],
            )
        return carry

    lax.fori_loop(0, (CELL_PLANES - 2) * ROWS // TILE, merge, 0)

    def relax(i, carry):
        for part in range(ROWS // TILE):
            base = pl.multiple_of(i * ROWS + part * TILE, TILE)
            here = base + ROWS + TILE
            rate = ratio[pl.ds(base, TILE), :]
            scale = 1.0 / (1.0 + 6.0 * rate)
            fringe = fringes[pl.ds(base, TILE), :] > 0.5
            for c in range(NV):
                mid = filled[c, pl.ds(pl.multiple_of(here, TILE), TILE), :]
                up = filled[c, pl.ds(here + 1, TILE), :]
                down = filled[c, pl.ds(here - 1, TILE), :]
                if part == 0:
                    down = jnp.where(level == 0, 0.0, down)
                if part == ROWS // TILE - 1:
                    up = jnp.where(level == TILE - 1, 0.0, up)
                left = jnp.where(lane == 0, 0.0, pltpu.roll(mid, 1, 1))
                right = jnp.where(lane == LANES - 1, 0.0, pltpu.roll(mid, LANES - 1, 1))
                total = (
                    filled[c, pl.ds(pl.multiple_of(here + ROWS, TILE), TILE), :]
                    + filled[c, pl.ds(pl.multiple_of(here - ROWS, TILE), TILE), :]
                    + up
                    + down
                    + left
                    + right
                )
                result[c, pl.ds(base, TILE), :] = jnp.where(
                    fringe, mid, (mid + rate * total) * scale
                )
        plane_out(i).start()
        return carry

    def plane_out(i):
        plane = pl.ds(pl.multiple_of(i * ROWS, ROWS), ROWS)
        return pltpu.make_async_copy(result.at[:, plane], out.at[:, plane], out_sem.at[i])

    lax.fori_loop(0, CELL_PLANES, relax, 0)
    for i in range(CELL_PLANES):
        plane_out(i).wait()


def fill_and_relax(counts, mark_rows, mark_groups, values, field, behind, ahead, ratio):
    owners = counts.shape[1]
    size = CELL_PLANES * ROWS
    hbm = pl.BlockSpec(memory_space=pltpu.HBM)
    f32 = jnp.float32
    return pl.pallas_call(
        fill_kernel,
        out_shape=jax.ShapeDtypeStruct(field.shape, f32),
        in_specs=[hbm] * 8,
        out_specs=hbm,
        scratch_shapes=[
            pltpu.SMEM((owners,), jnp.int32),
            pltpu.SMEM(mark_rows.shape, jnp.int32),
            pltpu.VMEM(mark_groups.shape, jnp.int32),
            pltpu.VMEM(values.shape, f32),
            pltpu.VMEM(field.shape, f32),
            pltpu.VMEM(behind.shape, f32),
            pltpu.VMEM(ahead.shape, f32),
            pltpu.VMEM(ratio.shape, f32),
            pltpu.VMEM((max((owners + 1) * LANES, FILL_ROWS), LANES), f32),
            pltpu.VMEM((FILL_ROWS + TILE, LANES), f32),
            pltpu.VMEM((NV, size + 2 * ROWS + 2 * TILE, LANES), f32),
            pltpu.VMEM((size, LANES), f32),
            pltpu.VMEM(field.shape, f32),
            pltpu.SemaphoreType.DMA((8,)),
            pltpu.SemaphoreType.DMA((CELL_PLANES,)),
        ],
        compiler_params=pltpu.CompilerParams(vmem_limit_bytes=62 << 20),
        name="fill",
    )(counts, mark_rows, mark_groups, values, field, behind, ahead, ratio)


def on_device(
    field, node_jitter, time_ratio, donor_cell, receptor_offset, receptor_node, point_count
):
    flat_field = field.reshape(NV, CELL_PLANES * ROWS, LANES)
    answers, ahead, behind, mark_rows, mark_groups = donor_values(
        donor_cell[0],
        jnp.moveaxis(receptor_offset[0], 2, 1),
        flat_field,
        node_jitter.reshape(3, CELL_PLANES * ROWS, LANES),
        receptor_node[0],
        point_count,
    )
    out = fill_and_relax(
        point_count,
        mark_rows,
        mark_groups,
        answers,
        flat_field,
        behind,
        ahead,
        time_ratio.reshape(CELL_PLANES * ROWS, LANES),
    )
    return out.reshape(field.shape)


def solution(mesh):
    placed = (
        P(None, ("grid", "sub"), None, None),
        P(None, ("grid", "sub"), None, None),
        P(("grid", "sub"), None, None),
        P(("grid", "sub"), None, None, None),
        P(("grid", "sub"), None, None, None, None),
        P(("grid", "sub"), None, None, None),
        P(("grid", "sub"), None),
    )
    return jax.shard_map(
        on_device,
        mesh=mesh,
        in_specs=placed,
        out_specs=P(None, ("grid", "sub"), None, None),
        check_vma=False,
    )
```

```python
import jax
import jax.numpy as jnp
from jax import lax
from jax.experimental import pallas as pl
from jax.experimental.pallas import tpu as pltpu
from jax.sharding import PartitionSpec as P

LANES = 128
TILE = 8
ROWS = 32
CELL_PLANES = 8
PLANE = ROWS * LANES
NV = 5
UNROLL = 64
HALF_CELLS = CELL_PLANES // 2 * PLANE
FILL_ROWS = (CELL_PLANES - 2) * PLANE // 16


def lerp(low, high, weight):
    return low + weight * (high - low)


def solve_group(places, target):
    size = target[0].shape
    param = [jnp.full(size, 0.5, jnp.float32) for _ in range(3)]
    rise = [
        [[places[m][a][b][1] - places[m][a][b][0] for b in range(2)] for a in range(2)]
        for m in range(3)
    ]
    for _ in range(4):
        u, v, w = param
        misfit, jac = [], []
        for m in range(3):
            edge = [[places[m][a][b][0] + w * rise[m][a][b] for b in range(2)] for a in range(2)]
            across = [edge[a][1] - edge[a][0] for a in range(2)]
            face = [edge[a][0] + v * across[a] for a in range(2)]
            slope0 = face[1] - face[0]
            misfit.append(face[0] + u * slope0 - target[m])
            slope1 = lerp(across[0], across[1], u)
            slope2 = lerp(
                lerp(rise[m][0][0], rise[m][0][1], v), lerp(rise[m][1][0], rise[m][1][1], v), u
            )
            jac.append((slope0, slope1, slope2))
        x, y, z = ([jac[m][d] for m in range(3)] for d in range(3))

        def cross(p, q):
            return [
                p[1] * q[2] - p[2] * q[1],
                p[2] * q[0] - p[0] * q[2],
                p[0] * q[1] - p[1] * q[0],
            ]

        def dot(p, q):
            return p[0] * q[0] + p[1] * q[1] + p[2] * q[2]

        yz, zx, xy = cross(y, z), cross(z, x), cross(x, y)
        inverse = 1.0 / dot(x, yz)
        param = [
            u - dot(misfit, yz) * inverse,
            v - dot(misfit, zx) * inverse,
            w - dot(misfit, xy) * inverse,
        ]
    return param


def wrap(index, count):
    return index & (count - 1) if count & (count - 1) == 0 else lax.rem(index, count)


def donor_kernel(
    cells_hbm, offsets_hbm, field, jitter, nodes, counts,
    answers, ahead_out, behind_out, mark_rows_out, mark_groups_out,
    cells, offsets, ahead, behind, mark_rows, mark_groups, counts_now, cells_in, cells_near, cells_now, offsets_in, field_here, jitter_here, tiles, shifted, table, picked, corners, sent,
    local_sems, halo_send, halo_recv, cell_send, cell_recv, offset_send, offset_recv,
    answer_send, answer_recv,
):
    grids = lax.axis_size("grid")
    subs = lax.axis_size("sub")
    me = lax.axis_index("grid")
    sub = lax.axis_index("sub")
    after, before = wrap(me + 1, grids), wrap(me + grids - 1, grids)
    sub_after, sub_before = wrap(sub + 1, subs), wrap(sub + subs - 1, subs)

    barrier = pltpu.get_barrier_semaphore()

    def greet(s, carry):
        pl.semaphore_signal(barrier, inc=1, device_id={"grid": wrap(me + s, grids)})
        return carry

    lax.fori_loop(1, grids, greet, 0, unroll=7)
    pl.semaphore_signal(barrier, inc=1, device_id={"sub": sub_after})
    pl.semaphore_signal(barrier, inc=1, device_id={"sub": sub_before})

    loads = [
        pltpu.make_async_copy(field, field_here, local_sems.at[0]),
        pltpu.make_async_copy(jitter, jitter_here, local_sems.at[1]),
        pltpu.make_async_copy(cells_hbm, cells, local_sems.at[5]),
        pltpu.make_async_copy(offsets_hbm, offsets, local_sems.at[6]),
    ]
    side_loads = [
        pltpu.make_async_copy(counts.at[0], counts_now, local_sems.at[2]),
        pltpu.make_async_copy(nodes.at[:, 0], mark_rows.at[pl.ds(0, grids)], local_sems.at[3]),
        pltpu.make_async_copy(nodes.at[after, 1], mark_rows.at[grids], local_sems.at[4]),
    ]
    for load in loads + side_loads:
        load.start()
    for load in loads:
        load.wait()

    def put(start, data):
        tiles[pl.ds(start, TILE, stride=TILE), :] = data
        shifted[pl.ds(start, TILE, stride=TILE), :] = pltpu.roll(data, LANES - 1, 1)

    def fill(tile, carry):
        base = pl.multiple_of(tile * TILE, TILE)
        for c in range(NV):
            put(base * TILE + c, field_here[c, pl.ds(base, TILE), :])
        for c in range(3):
            put(base * TILE + NV + c, jitter_here[c, pl.ds(base, TILE), :])
        return carry

    lax.fori_loop(0, CELL_PLANES * ROWS // TILE, fill, 0)
    pl.semaphore_wait(barrier, grids + 1)

    def remote(source, target, send, recv, device):
        return pltpu.make_async_remote_copy(
            src_ref=source, dst_ref=target, send_sem=send, recv_sem=recv, device_id=device
        )

    first, last = pl.ds(0, ROWS), pl.ds((CELL_PLANES - 1) * ROWS, ROWS)
    halos = [
        remote(
            field_here.at[:, first], ahead.at[pl.ds(0, NV)],
            halo_send.at[0], halo_recv.at[0], {"sub": sub_before},
        ),
        remote(
            jitter_here.at[:, first], ahead.at[pl.ds(NV, 3)],
            halo_send.at[1], halo_recv.at[1], {"sub": sub_before},
        ),
        remote(
            field_here.at[:, last], behind, halo_send.at[2], halo_recv.at[2], {"sub": sub_after}
        ),
    ]
    for halo in halos:
        halo.start()

    def cell_copy(peer):
        return remote(
            cells.at[peer, 0], cells_in.at[me], cell_send.at[0], cell_recv.at[0], {"grid": peer}
        )

    def offset_copy(peer):
        return remote(
            offsets.at[peer, :, 0], offsets_in.at[pl.ds(me * TILE, 3)],
            offset_send.at[0], offset_recv.at[0], {"grid": peer},
        )

    def send_cells(s, carry):
        cell_copy(wrap(me + s, grids)).start()
        return carry

    def send_offsets(s, carry):
        offset_copy(wrap(me + s, grids)).start()
        return carry

    lax.fori_loop(1, grids, send_cells, 0, unroll=7)
    more_cells = remote(
        cells.at[after, 1], cells_in.at[grids], cell_send.at[1], cell_recv.at[1], {"grid": after}
    )
    more_cells.start()
    own_cells = pltpu.make_async_copy(cells.at[me, 0], cells_in.at[me], local_sems.at[0])
    own_cells.start()
    lax.fori_loop(1, grids, send_offsets, 0, unroll=7)
    more_offsets = remote(
        offsets.at[after, :, 1], offsets_in.at[pl.ds(grids * TILE, 3)],
        offset_send.at[1], offset_recv.at[1], {"grid": after},
    )
    more_offsets.start()
    own_offsets = pltpu.make_async_copy(
        offsets.at[me, :, 0], offsets_in.at[pl.ds(me * TILE, 3)], local_sems.at[1]
    )
    own_offsets.start()

    for load in side_loads:
        load.wait()
    slot = lax.broadcasted_iota(jnp.int32, (1, LANES), 1)

    def mark(o, live):
        node = mark_rows[pl.ds(o, 1), :]
        place = (((node >> 11) - 2) << 7) + (node & (LANES - 1))
        mark_rows[pl.ds(o, 1), :] = jnp.where(slot < live, place, FILL_ROWS)
        mark_groups[pl.ds(o, 1), :] = (node >> 7) & 15

    def mark_step(o, carry):
        mark(o, counts_now[o])
        return carry

    lax.fori_loop(0, grids, mark_step, 0)
    mark(grids, counts_now[after] - LANES)
    stores = [
        pltpu.make_async_copy(mark_rows, mark_rows_out, local_sems.at[3]),
        pltpu.make_async_copy(mark_groups, mark_groups_out, local_sems.at[4]),
        pltpu.make_async_copy(ahead, ahead_out, local_sems.at[5]),
        pltpu.make_async_copy(behind, behind_out, local_sems.at[6]),
    ]
    stores[0].start()
    stores[1].start()

    def build_some(q, carry):
        for step in range(4):
            row = q * 4 + step
            parts = []
            for half in range(2):
                for a in (0, 1, ROWS, ROWS + 1):
                    start = (row + half * (CELL_PLANES // 2) * ROWS + a) * TILE
                    start = pl.multiple_of(start, TILE)
                    parts.append(tiles[pl.ds(start, TILE), :])
                    parts.append(shifted[pl.ds(start, TILE), :])
            table[pl.ds(pl.multiple_of(row * LANES, LANES), LANES), :] = jnp.concatenate(
                parts, 0
            ).T
        return carry

    quarter = ROWS // 4
    lax.fori_loop(0, 3 * quarter, build_some, 0)
    for halo in halos:
        halo.wait_recv()
    stores[2].start()
    stores[3].start()
    for tile in range(ROWS // TILE):
        for c in range(8):
            put(
                (CELL_PLANES * ROWS + tile * TILE) * TILE + c,
                ahead[c, pl.ds(tile * TILE, TILE), :],
            )

    def drain(buffer, sem):
        pltpu.make_async_copy(buffer, buffer, sem).wait()

    drain(cells_in.at[pl.ds(0, grids - 1)], cell_recv.at[0])
    own_cells.wait()
    more_cells.wait_recv()
    cells_near[...] = cells_in[...] & (HALF_CELLS - 1)
    load_cells = pltpu.make_async_copy(cells_near, cells_now, local_sems.at[0])
    load_cells.start()
    lax.fori_loop(3 * quarter, 4 * quarter, build_some, 0)
    load_cells.wait()

    def pick(block, count):
        def one(r, carry):
            to = pl.multiple_of(r * LANES, LANES)
            for t in range(LANES):
                picked[pl.ds(to + t, 1), :] = table[pl.ds(cells_now[block + r, t], 1), :]
            return carry

        lax.fori_loop(0, count, one, 0, unroll=min(count, 2))

    def turn(block, r):
        values = picked[r * LANES : (r + 1) * LANES, :].T
        far = cells_in[pl.ds(block + r, 1), :] >= HALF_CELLS
        for q in range(8):
            corners[q, r * TILE : (r + 1) * TILE, :] = jnp.where(
                far, values[64 + 8 * q : 72 + 8 * q], values[8 * q : 8 * q + 8]
            )

    def solve(block):
        target = [
            offsets_in[pl.ds(block * TILE + m, TILE, stride=TILE), :] for m in range(3)
        ]
        places = [
            [
                [
                    [
                        corners[4 * a + 2 * b + d, pl.ds(NV + m, TILE, stride=TILE), :]
                        + float((a, b, d)[m])
                        for d in range(2)
                    ]
                    for b in range(2)
                ]
                for a in range(2)
            ]
            for m in range(3)
        ]
        u, v, w = solve_group(places, target)
        for c in range(NV):
            node = [corners[q, pl.ds(c, TILE, stride=TILE), :] for q in range(8)]
            edge = [lerp(node[2 * e], node[2 * e + 1], w) for e in range(4)]
            value = lerp(lerp(edge[0], edge[1], v), lerp(edge[2], edge[3], v), u)
            sent[pl.ds(block * TILE + c, TILE, stride=TILE), :] = value

    own_answer = pltpu.make_async_copy(
        sent.at[pl.ds(me * TILE, NV)], answers.at[pl.ds(me * TILE, NV)], local_sems.at[0]
    )

    def group(g, carry):
        block = pl.multiple_of(wrap((me >> 3) + g, grids // TILE) * TILE, TILE)
        pick(block, TILE)
        for r in range(TILE):
            turn(block, r)
        @pl.when(g == 0)
        def _():
            drain(picked.at[pl.ds(0, 3 * (grids - 1))], offset_recv.at[0])
            own_offsets.wait()
            more_offsets.wait_recv()

        solve(block)

        for r in range(TILE):
            peer = block + r

            @pl.when(peer != me)
            def _():
                remote(
                    sent.at[pl.ds(peer * TILE, NV)], answers.at[pl.ds(me * TILE, NV)],
                    answer_send.at[0], answer_recv.at[0], {"grid": peer},
                ).start()

            @pl.when(peer == me)
            def _():
                own_answer.start()

        return carry

    lax.fori_loop(0, grids // TILE, group, 0)
    pick(grids, 1)
    turn(grids, 0)
    solve(grids)
    more_answers = remote(
        sent.at[pl.ds(grids * TILE, NV)], answers.at[pl.ds(grids * TILE, NV)],
        answer_send.at[1], answer_recv.at[1], {"grid": before},
    )
    more_answers.start()

    drain(picked.at[pl.ds(0, NV * (grids - 1))], answer_recv.at[0])
    own_answer.wait()
    more_answers.wait()
    drain(picked.at[pl.ds(0, NV * (grids - 1))], answer_send.at[0])
    drain(cells_in.at[pl.ds(0, grids - 1)], cell_send.at[0])
    drain(picked.at[pl.ds(0, 3 * (grids - 1))], offset_send.at[0])
    more_cells.wait_send()
    more_offsets.wait_send()
    for halo in halos:
        halo.wait_send()
    for store in stores:
        store.wait()


def donor_values(cells, offsets, field, jitter, nodes, counts):
    grids = cells.shape[0]
    padded = grids + TILE
    node_rows = (CELL_PLANES + 1) * ROWS
    hbm = pl.BlockSpec(memory_space=pltpu.HBM)
    f32 = jnp.float32
    return pl.pallas_call(
        donor_kernel,
        out_shape=(
            jax.ShapeDtypeStruct(((grids + 1) * TILE, LANES), f32),
            jax.ShapeDtypeStruct((8, ROWS, LANES), f32),
            jax.ShapeDtypeStruct((NV, ROWS, LANES), f32),
            jax.ShapeDtypeStruct((padded, LANES), jnp.int32),
            jax.ShapeDtypeStruct((padded, LANES), jnp.int32),
        ),
        in_specs=[hbm] * 6,
        out_specs=(hbm,) * 5,
        scratch_shapes=[
            pltpu.VMEM(cells.shape, jnp.int32),
            pltpu.VMEM(offsets.shape, f32),
            pltpu.VMEM((8, ROWS, LANES), f32),
            pltpu.VMEM((NV, ROWS, LANES), f32),
            pltpu.VMEM((padded, LANES), jnp.int32),
            pltpu.VMEM((padded, LANES), jnp.int32),
            pltpu.SMEM((grids,), jnp.int32),
            pltpu.VMEM((padded, LANES), jnp.int32),
            pltpu.VMEM((padded, LANES), jnp.int32),
            pltpu.SMEM((padded, LANES), jnp.int32),
            pltpu.VMEM((padded * TILE, LANES), f32),
            pltpu.VMEM(field.shape, f32),
            pltpu.VMEM(jitter.shape, f32),
            pltpu.VMEM((node_rows * TILE + 2 * TILE, LANES), f32),
            pltpu.VMEM((node_rows * TILE + 2 * TILE, LANES), f32),
            pltpu.VMEM((HALF_CELLS, LANES), f32),
            pltpu.VMEM((TILE * LANES, LANES), f32),
            pltpu.VMEM((8, TILE * TILE, LANES), f32),
            pltpu.VMEM((padded * TILE, LANES), f32),
        ]
        + [pltpu.SemaphoreType.DMA((n,)) for n in (7, 3, 3, 2, 2, 2, 2, 2, 2)],
        compiler_params=pltpu.CompilerParams(
            collective_id=0, has_side_effects=True, vmem_limit_bytes=60 << 20
        ),
        name="donor",
    )(cells, offsets, field, jitter, nodes, counts)


def fill_kernel(
    counts_in, mark_rows_in, mark_groups_in, values_in, field_in, behind_in, ahead_in, ratio_in, out,
    counts, mark_rows, mark_groups, values, field, behind, ahead, ratio,
    turned, rows, filled, fringes, result, sems, out_sem,
):
    owners = counts.shape[0]
    loads = [
        pltpu.make_async_copy(source, target, sems.at[n])
        for n, (source, target) in enumerate(
            (
                (values_in, values),
                (mark_rows_in, mark_rows),
                (mark_groups_in, mark_groups),
                (counts_in.at[0], counts),
                (field_in, field),
                (behind_in, behind),
                (ahead_in, ahead),
                (ratio_in, ratio),
            )
        )
    ]
    for load in loads:
        load.start()
    size = CELL_PLANES * ROWS
    lane = lax.broadcasted_iota(jnp.int32, (TILE, LANES), 1)
    level = lax.broadcasted_iota(jnp.int32, (TILE, LANES), 0)

    def clear(q, carry):
        rows[pl.ds(pl.multiple_of(q * LANES, LANES), LANES), :] = jnp.zeros(
            (LANES, LANES), jnp.float32
        )
        return carry

    lax.fori_loop(0, FILL_ROWS // LANES, clear, 0)
    loads[0].wait()
    loads[2].wait()

    def spread(o):
        block = values[pl.ds(pl.multiple_of(o * TILE, TILE), TILE), :]
        block = jnp.where(level < NV, block, 1.0)
        choice = jnp.broadcast_to(mark_groups[pl.ds(o, 1), :], (TILE, LANES))
        parts = [jnp.where(choice == g, block, jnp.inf) for g in range(16)]
        start = pl.multiple_of(o * LANES, LANES)
        turned[pl.ds(start, LANES), :] = jnp.concatenate(parts, 0).T

    def spread_some(g, carry):
        for step in range(16):
            spread(g * 16 + step)
        return carry

    lax.fori_loop(0, owners // 16, spread_some, 0)
    spread(owners)

    loads[1].wait()
    loads[3].wait()

    def scatter(o, live):
        first = pl.multiple_of(o * LANES, LANES)
        for start in range(0, LANES, UNROLL):

            @pl.when(live > start)
            def _():
                for t in range(start, start + UNROLL):
                    row = turned[pl.ds(first + t, 1), :]
                    pltpu.store(
                        rows.at[pl.ds(mark_rows[o, t], 1), :], row, mask=row < jnp.inf
                    )

    def scatter_step(o, carry):
        scatter(o, jnp.minimum(counts[o], LANES))
        return carry

    lax.fori_loop(0, owners, scatter_step, 0)
    scatter(owners, LANES)

    def back(q):
        start = pl.multiple_of(q * LANES, LANES)
        turned[pl.ds(start, LANES), :] = rows[pl.ds(start, LANES), :].T

    def back_some(g, carry):
        for step in range(4):
            back(g * 4 + step)
        return carry

    lax.fori_loop(0, FILL_ROWS // LANES // 4, back_some, 0)

    for load in loads[4:]:
        load.wait()

    for c in range(NV):
        filled[c, 0:TILE, :] = jnp.zeros((TILE, LANES), jnp.float32)
        for plane, data in (
            (0, behind[c]),
            (1, field[c, 0:ROWS, :]),
            (CELL_PLANES, field[c, size - ROWS : size, :]),
            (CELL_PLANES + 1, ahead[c]),
        ):
            filled[c, TILE + plane * ROWS : TILE + (plane + 1) * ROWS, :] = data
    for edge in (0, size - ROWS):
        fringes[edge : edge + ROWS, :] = jnp.zeros((ROWS, LANES), jnp.float32)

    def merge(tile, carry):
        base = pl.multiple_of(tile * TILE, TILE)
        inner = pl.multiple_of(base + ROWS, TILE)
        flag = turned[pl.ds(base * TILE + NV, TILE, stride=TILE), :]
        fringes[pl.ds(inner, TILE), :] = flag
        for c in range(NV):
            filled[c, pl.ds(pl.multiple_of(inner + ROWS + TILE, TILE), TILE), :] = jnp.where(
                flag > 0.5,
                turned[pl.ds(base * TILE + c, TILE, stride=TILE), :],
                field[c, pl.ds(inner, TILE), :],
            )
        return carry

    lax.fori_loop(0, (CELL_PLANES - 2) * ROWS // TILE, merge, 0)

    def relax(i, carry):
        for part in range(ROWS // TILE):
            base = pl.multiple_of(i * ROWS + part * TILE, TILE)
            here = base + ROWS + TILE
            rate = ratio[pl.ds(base, TILE), :]
            scale = 1.0 / (1.0 + 6.0 * rate)
            fringe = fringes[pl.ds(base, TILE), :] > 0.5
            for c in range(NV):
                mid = filled[c, pl.ds(pl.multiple_of(here, TILE), TILE), :]
                up = filled[c, pl.ds(here + 1, TILE), :]
                down = filled[c, pl.ds(here - 1, TILE), :]
                if part == 0:
                    down = jnp.where(level == 0, 0.0, down)
                if part == ROWS // TILE - 1:
                    up = jnp.where(level == TILE - 1, 0.0, up)
                left = jnp.where(lane == 0, 0.0, pltpu.roll(mid, 1, 1))
                right = jnp.where(lane == LANES - 1, 0.0, pltpu.roll(mid, LANES - 1, 1))
                total = (
                    filled[c, pl.ds(pl.multiple_of(here + ROWS, TILE), TILE), :]
                    + filled[c, pl.ds(pl.multiple_of(here - ROWS, TILE), TILE), :]
                    + up
                    + down
                    + left
                    + right
                )
                result[c, pl.ds(base, TILE), :] = jnp.where(
                    fringe, mid, (mid + rate * total) * scale
                )
        plane_out(i).start()
        return carry

    def plane_out(i):
        plane = pl.ds(pl.multiple_of(i * ROWS, ROWS), ROWS)
        return pltpu.make_async_copy(result.at[:, plane], out.at[:, plane], out_sem.at[i])

    lax.fori_loop(0, CELL_PLANES, relax, 0)
    for i in range(CELL_PLANES):
        plane_out(i).wait()


def fill_and_relax(counts, mark_rows, mark_groups, values, field, behind, ahead, ratio):
    owners = counts.shape[1]
    size = CELL_PLANES * ROWS
    hbm = pl.BlockSpec(memory_space=pltpu.HBM)
    f32 = jnp.float32
    return pl.pallas_call(
        fill_kernel,
        out_shape=jax.ShapeDtypeStruct(field.shape, f32),
        in_specs=[hbm] * 8,
        out_specs=hbm,
        scratch_shapes=[
            pltpu.SMEM((owners,), jnp.int32),
            pltpu.SMEM(mark_rows.shape, jnp.int32),
            pltpu.VMEM(mark_groups.shape, jnp.int32),
            pltpu.VMEM(values.shape, f32),
            pltpu.VMEM(field.shape, f32),
            pltpu.VMEM(behind.shape, f32),
            pltpu.VMEM(ahead.shape, f32),
            pltpu.VMEM(ratio.shape, f32),
            pltpu.VMEM((max((owners + 1) * LANES, FILL_ROWS), LANES), f32),
            pltpu.VMEM((FILL_ROWS + TILE, LANES), f32),
            pltpu.VMEM((NV, size + 2 * ROWS + 2 * TILE, LANES), f32),
            pltpu.VMEM((size, LANES), f32),
            pltpu.VMEM(field.shape, f32),
            pltpu.SemaphoreType.DMA((8,)),
            pltpu.SemaphoreType.DMA((CELL_PLANES,)),
        ],
        compiler_params=pltpu.CompilerParams(vmem_limit_bytes=62 << 20),
        name="fill",
    )(counts, mark_rows, mark_groups, values, field, behind, ahead, ratio)


def on_device(
    field, node_jitter, time_ratio, donor_cell, receptor_offset, receptor_node, point_count
):
    flat_field = field.reshape(NV, CELL_PLANES * ROWS, LANES)
    answers, ahead, behind, mark_rows, mark_groups = donor_values(
        donor_cell[0],
        jnp.moveaxis(receptor_offset[0], 2, 1),
        flat_field,
        node_jitter.reshape(3, CELL_PLANES * ROWS, LANES),
        receptor_node[0],
        point_count,
    )
    out = fill_and_relax(
        point_count,
        mark_rows,
        mark_groups,
        answers,
        flat_field,
        behind,
        ahead,
        time_ratio.reshape(CELL_PLANES * ROWS, LANES),
    )
    return out.reshape(field.shape)


def solution(mesh):
    placed = (
        P(None, ("grid", "sub"), None, None),
        P(None, ("grid", "sub"), None, None),
        P(("grid", "sub"), None, None),
        P(("grid", "sub"), None, None, None),
        P(("grid", "sub"), None, None, None, None),
        P(("grid", "sub"), None, None, None),
        P(("grid", "sub"), None),
    )
    return jax.shard_map(
        on_device,
        mesh=mesh,
        in_specs=placed,
        out_specs=P(None, ("grid", "sub"), None, None),
        check_vma=False,
    )
```

```python
import jax
import jax.numpy as jnp
from jax import lax
from jax.experimental import pallas as pl
from jax.experimental.pallas import tpu as pltpu
from jax.sharding import PartitionSpec as P

LANES = 128
TILE = 8
ROWS = 32
CELL_PLANES = 8
PLANE = ROWS * LANES
NV = 5
UNROLL = 64
HALF_CELLS = CELL_PLANES // 2 * PLANE
FILL_ROWS = (CELL_PLANES - 2) * PLANE // 16


def lerp(low, high, weight):
    return low + weight * (high - low)


def solve_group(places, target):
    size = target[0].shape
    param = [jnp.full(size, 0.5, jnp.float32) for _ in range(3)]
    rise = [
        [[places[m][a][b][1] - places[m][a][b][0] for b in range(2)] for a in range(2)]
        for m in range(3)
    ]
    for _ in range(4):
        u, v, w = param
        misfit, jac = [], []
        for m in range(3):
            edge = [[places[m][a][b][0] + w * rise[m][a][b] for b in range(2)] for a in range(2)]
            across = [edge[a][1] - edge[a][0] for a in range(2)]
            face = [edge[a][0] + v * across[a] for a in range(2)]
            slope0 = face[1] - face[0]
            misfit.append(face[0] + u * slope0 - target[m])
            slope1 = lerp(across[0], across[1], u)
            slope2 = lerp(
                lerp(rise[m][0][0], rise[m][0][1], v), lerp(rise[m][1][0], rise[m][1][1], v), u
            )
            jac.append((slope0, slope1, slope2))
        x, y, z = ([jac[m][d] for m in range(3)] for d in range(3))

        def cross(p, q):
            return [
                p[1] * q[2] - p[2] * q[1],
                p[2] * q[0] - p[0] * q[2],
                p[0] * q[1] - p[1] * q[0],
            ]

        def dot(p, q):
            return p[0] * q[0] + p[1] * q[1] + p[2] * q[2]

        yz, zx, xy = cross(y, z), cross(z, x), cross(x, y)
        inverse = 1.0 / dot(x, yz)
        param = [
            u - dot(misfit, yz) * inverse,
            v - dot(misfit, zx) * inverse,
            w - dot(misfit, xy) * inverse,
        ]
    return param


def wrap(index, count):
    return index & (count - 1) if count & (count - 1) == 0 else lax.rem(index, count)


def donor_kernel(
    cells_hbm, offsets_hbm, field, jitter, nodes, counts,
    answers, ahead_out, behind_out, mark_rows_out, mark_groups_out,
    cells, offsets, ahead, behind, mark_rows, mark_groups, counts_now, cells_in, cells_near, cells_now, offsets_in, field_here, jitter_here, tiles, shifted, table, picked, corners, sent,
    local_sems, halo_send, halo_recv, cell_send, cell_recv, offset_send, offset_recv,
    answer_send, answer_recv,
):
    grids = lax.axis_size("grid")
    subs = lax.axis_size("sub")
    me = lax.axis_index("grid")
    sub = lax.axis_index("sub")
    after, before = wrap(me + 1, grids), wrap(me + grids - 1, grids)
    sub_after, sub_before = wrap(sub + 1, subs), wrap(sub + subs - 1, subs)

    barrier = pltpu.get_barrier_semaphore()

    def greet(s, carry):
        pl.semaphore_signal(barrier, inc=1, device_id={"grid": wrap(me + s, grids)})
        return carry

    lax.fori_loop(1, grids, greet, 0, unroll=7)
    pl.semaphore_signal(barrier, inc=1, device_id={"sub": sub_after})
    pl.semaphore_signal(barrier, inc=1, device_id={"sub": sub_before})

    loads = [
        pltpu.make_async_copy(field, field_here, local_sems.at[0]),
        pltpu.make_async_copy(jitter, jitter_here, local_sems.at[1]),
        pltpu.make_async_copy(cells_hbm, cells, local_sems.at[5]),
        pltpu.make_async_copy(offsets_hbm, offsets, local_sems.at[6]),
    ]
    side_loads = [
        pltpu.make_async_copy(counts.at[0], counts_now, local_sems.at[2]),
        pltpu.make_async_copy(nodes.at[:, 0], mark_rows.at[pl.ds(0, grids)], local_sems.at[3]),
        pltpu.make_async_copy(nodes.at[after, 1], mark_rows.at[grids], local_sems.at[4]),
    ]
    for load in loads + side_loads:
        load.start()
    for load in loads:
        load.wait()

    def put(start, data):
        tiles[pl.ds(start, TILE, stride=TILE), :] = data
        shifted[pl.ds(start, TILE, stride=TILE), :] = pltpu.roll(data, LANES - 1, 1)

    def fill(tile, carry):
        base = pl.multiple_of(tile * TILE, TILE)
        for c in range(NV):
            put(base * TILE + c, field_here[c, pl.ds(base, TILE), :])
        for c in range(3):
            put(base * TILE + NV + c, jitter_here[c, pl.ds(base, TILE), :])
        return carry

    lax.fori_loop(0, CELL_PLANES * ROWS // TILE, fill, 0)
    pl.semaphore_wait(barrier, grids + 1)

    def remote(source, target, send, recv, device):
        return pltpu.make_async_remote_copy(
            src_ref=source, dst_ref=target, send_sem=send, recv_sem=recv, device_id=device
        )

    first, last = pl.ds(0, ROWS), pl.ds((CELL_PLANES - 1) * ROWS, ROWS)
    halos = [
        remote(
            field_here.at[:, first], ahead.at[pl.ds(0, NV)],
            halo_send.at[0], halo_recv.at[0], {"sub": sub_before},
        ),
        remote(
            jitter_here.at[:, first], ahead.at[pl.ds(NV, 3)],
            halo_send.at[1], halo_recv.at[1], {"sub": sub_before},
        ),
        remote(
            field_here.at[:, last], behind, halo_send.at[2], halo_recv.at[2], {"sub": sub_after}
        ),
    ]
    for halo in halos:
        halo.start()

    def cell_copy(peer):
        return remote(
            cells.at[peer, 0], cells_in.at[me], cell_send.at[0], cell_recv.at[0], {"grid": peer}
        )

    def offset_copy(peer):
        return remote(
            offsets.at[peer, :, 0], offsets_in.at[pl.ds(me * TILE, 3)],
            offset_send.at[0], offset_recv.at[0], {"grid": peer},
        )

    def send_cells(s, carry):
        cell_copy(wrap(me + s, grids)).start()
        return carry

    def send_offsets(s, carry):
        offset_copy(wrap(me + s, grids)).start()
        return carry

    lax.fori_loop(1, grids, send_cells, 0, unroll=7)
    more_cells = remote(
        cells.at[after, 1], cells_in.at[grids], cell_send.at[1], cell_recv.at[1], {"grid": after}
    )
    more_cells.start()
    own_cells = pltpu.make_async_copy(cells.at[me, 0], cells_in.at[me], local_sems.at[0])
    own_cells.start()
    lax.fori_loop(1, grids, send_offsets, 0, unroll=7)
    more_offsets = remote(
        offsets.at[after, :, 1], offsets_in.at[pl.ds(grids * TILE, 3)],
        offset_send.at[1], offset_recv.at[1], {"grid": after},
    )
    more_offsets.start()
    own_offsets = pltpu.make_async_copy(
        offsets.at[me, :, 0], offsets_in.at[pl.ds(me * TILE, 3)], local_sems.at[1]
    )
    own_offsets.start()

    for load in side_loads:
        load.wait()
    slot = lax.broadcasted_iota(jnp.int32, (1, LANES), 1)

    def mark(o, live):
        node = mark_rows[pl.ds(o, 1), :]
        place = (((node >> 11) - 2) << 7) + (node & (LANES - 1))
        mark_rows[pl.ds(o, 1), :] = jnp.where(slot < live, place, FILL_ROWS)
        mark_groups[pl.ds(o, 1), :] = (node >> 7) & 15

    def mark_step(o, carry):
        mark(o, counts_now[o])
        return carry

    lax.fori_loop(0, grids, mark_step, 0)
    mark(grids, counts_now[after] - LANES)
    stores = [
        pltpu.make_async_copy(mark_rows, mark_rows_out, local_sems.at[3]),
        pltpu.make_async_copy(mark_groups, mark_groups_out, local_sems.at[4]),
        pltpu.make_async_copy(ahead, ahead_out, local_sems.at[5]),
        pltpu.make_async_copy(behind, behind_out, local_sems.at[6]),
    ]
    stores[0].start()
    stores[1].start()

    def build_some(q, carry):
        for step in range(4):
            row = q * 4 + step
            parts = []
            for half in range(2):
                for a in (0, 1, ROWS, ROWS + 1):
                    start = (row + half * (CELL_PLANES // 2) * ROWS + a) * TILE
                    start = pl.multiple_of(start, TILE)
                    parts.append(tiles[pl.ds(start, TILE), :])
                    parts.append(shifted[pl.ds(start, TILE), :])
            table[pl.ds(pl.multiple_of(row * LANES, LANES), LANES), :] = jnp.concatenate(
                parts, 0
            ).T
        return carry

    quarter = ROWS // 4
    lax.fori_loop(0, 3 * quarter, build_some, 0)
    for halo in halos:
        halo.wait_recv()
    stores[2].start()
    stores[3].start()
    for tile in range(ROWS // TILE):
        for c in range(8):
            put(
                (CELL_PLANES * ROWS + tile * TILE) * TILE + c,
                ahead[c, pl.ds(tile * TILE, TILE), :],
            )

    def drain(buffer, sem):
        pltpu.make_async_copy(buffer, buffer, sem).wait()

    drain(cells_in.at[pl.ds(0, grids - 1)], cell_recv.at[0])
    own_cells.wait()
    more_cells.wait_recv()
    cells_near[...] = cells_in[...] & (HALF_CELLS - 1)
    load_cells = pltpu.make_async_copy(cells_near, cells_now, local_sems.at[0])
    load_cells.start()
    lax.fori_loop(3 * quarter, 4 * quarter, build_some, 0)
    load_cells.wait()

    def pick(block, count):
        def one(r, carry):
            to = pl.multiple_of(r * LANES, LANES)
            for t in range(LANES):
                picked[pl.ds(to + t, 1), :] = table[pl.ds(cells_now[block + r, t], 1), :]
            return carry

        lax.fori_loop(0, count, one, 0, unroll=min(count, 2))

    def turn(block, r):
        values = picked[r * LANES : (r + 1) * LANES, :].T
        far = cells_in[pl.ds(block + r, 1), :] >= HALF_CELLS
        for q in range(8):
            corners[q, r * TILE : (r + 1) * TILE, :] = jnp.where(
                far, values[64 + 8 * q : 72 + 8 * q], values[8 * q : 8 * q + 8]
            )

    def solve(block):
        target = [
            offsets_in[pl.ds(block * TILE + m, TILE, stride=TILE), :] for m in range(3)
        ]
        places = [
            [
                [
                    [
                        corners[4 * a + 2 * b + d, pl.ds(NV + m, TILE, stride=TILE), :]
                        + float((a, b, d)[m])
                        for d in range(2)
                    ]
                    for b in range(2)
                ]
                for a in range(2)
            ]
            for m in range(3)
        ]
        u, v, w = solve_group(places, target)
        for c in range(NV):
            node = [corners[q, pl.ds(c, TILE, stride=TILE), :] for q in range(8)]
            edge = [lerp(node[2 * e], node[2 * e + 1], w) for e in range(4)]
            value = lerp(lerp(edge[0], edge[1], v), lerp(edge[2], edge[3], v), u)
            sent[pl.ds(block * TILE + c, TILE, stride=TILE), :] = value

    own_answer = pltpu.make_async_copy(
        sent.at[pl.ds(me * TILE, NV)], answers.at[pl.ds(me * TILE, NV)], local_sems.at[0]
    )

    def group(g, carry):
        block = pl.multiple_of(wrap((me >> 3) + g, grids // TILE) * TILE, TILE)
        pick(block, TILE)
        for r in range(TILE):
            turn(block, r)
        @pl.when(g == 0)
        def _():
            drain(picked.at[pl.ds(0, 3 * (grids - 1))], offset_recv.at[0])
            own_offsets.wait()
            more_offsets.wait_recv()

        solve(block)

        for r in range(TILE):
            peer = block + r

            @pl.when(peer != me)
            def _():
                remote(
                    sent.at[pl.ds(peer * TILE, NV)], answers.at[pl.ds(me * TILE, NV)],
                    answer_send.at[0], answer_recv.at[0], {"grid": peer},
                ).start()

            @pl.when(peer == me)
            def _():
                own_answer.start()

        return carry

    lax.fori_loop(0, grids // TILE, group, 0)
    pick(grids, 1)
    turn(grids, 0)
    solve(grids)
    more_answers = remote(
        sent.at[pl.ds(grids * TILE, NV)], answers.at[pl.ds(grids * TILE, NV)],
        answer_send.at[1], answer_recv.at[1], {"grid": before},
    )
    more_answers.start()

    drain(picked.at[pl.ds(0, NV * (grids - 1))], answer_recv.at[0])
    own_answer.wait()
    more_answers.wait()
    drain(picked.at[pl.ds(0, NV * (grids - 1))], answer_send.at[0])
    drain(cells_in.at[pl.ds(0, grids - 1)], cell_send.at[0])
    drain(picked.at[pl.ds(0, 3 * (grids - 1))], offset_send.at[0])
    more_cells.wait_send()
    more_offsets.wait_send()
    for halo in halos:
        halo.wait_send()
    for store in stores:
        store.wait()


def donor_values(cells, offsets, field, jitter, nodes, counts):
    grids = cells.shape[0]
    padded = grids + TILE
    node_rows = (CELL_PLANES + 1) * ROWS
    hbm = pl.BlockSpec(memory_space=pltpu.HBM)
    f32 = jnp.float32
    return pl.pallas_call(
        donor_kernel,
        out_shape=(
            jax.ShapeDtypeStruct(((grids + 1) * TILE, LANES), f32),
            jax.ShapeDtypeStruct((8, ROWS, LANES), f32),
            jax.ShapeDtypeStruct((NV, ROWS, LANES), f32),
            jax.ShapeDtypeStruct((padded, LANES), jnp.int32),
            jax.ShapeDtypeStruct((padded, LANES), jnp.int32),
        ),
        in_specs=[hbm] * 6,
        out_specs=(hbm,) * 5,
        scratch_shapes=[
            pltpu.VMEM(cells.shape, jnp.int32),
            pltpu.VMEM(offsets.shape, f32),
            pltpu.VMEM((8, ROWS, LANES), f32),
            pltpu.VMEM((NV, ROWS, LANES), f32),
            pltpu.VMEM((padded, LANES), jnp.int32),
            pltpu.VMEM((padded, LANES), jnp.int32),
            pltpu.SMEM((grids,), jnp.int32),
            pltpu.VMEM((padded, LANES), jnp.int32),
            pltpu.VMEM((padded, LANES), jnp.int32),
            pltpu.SMEM((padded, LANES), jnp.int32),
            pltpu.VMEM((padded * TILE, LANES), f32),
            pltpu.VMEM(field.shape, f32),
            pltpu.VMEM(jitter.shape, f32),
            pltpu.VMEM((node_rows * TILE + 2 * TILE, LANES), f32),
            pltpu.VMEM((node_rows * TILE + 2 * TILE, LANES), f32),
            pltpu.VMEM((HALF_CELLS, LANES), f32),
            pltpu.VMEM((TILE * LANES, LANES), f32),
            pltpu.VMEM((8, TILE * TILE, LANES), f32),
            pltpu.VMEM((padded * TILE, LANES), f32),
        ]
        + [pltpu.SemaphoreType.DMA((n,)) for n in (7, 3, 3, 2, 2, 2, 2, 2, 2)],
        compiler_params=pltpu.CompilerParams(
            collective_id=0, has_side_effects=True, vmem_limit_bytes=60 << 20
        ),
        name="donor",
    )(cells, offsets, field, jitter, nodes, counts)


def fill_kernel(
    counts_in, mark_rows_in, mark_groups_in, values_in, field_in, behind_in, ahead_in, ratio_in, out,
    counts, mark_rows, mark_groups, values, field, behind, ahead, ratio,
    turned, rows, filled, fringes, result, sems, out_sem,
):
    owners = counts.shape[0]
    loads = [
        pltpu.make_async_copy(source, target, sems.at[n])
        for n, (source, target) in enumerate(
            (
                (values_in, values),
                (mark_rows_in, mark_rows),
                (mark_groups_in, mark_groups),
                (counts_in.at[0], counts),
                (field_in, field),
                (behind_in, behind),
                (ahead_in, ahead),
                (ratio_in, ratio),
            )
        )
    ]
    for load in loads:
        load.start()
    size = CELL_PLANES * ROWS
    lane = lax.broadcasted_iota(jnp.int32, (TILE, LANES), 1)
    level = lax.broadcasted_iota(jnp.int32, (TILE, LANES), 0)

    def clear(q, carry):
        rows[pl.ds(pl.multiple_of(q * LANES, LANES), LANES), :] = jnp.zeros(
            (LANES, LANES), jnp.float32
        )
        return carry

    lax.fori_loop(0, FILL_ROWS // LANES, clear, 0)
    loads[0].wait()
    loads[2].wait()

    def spread(o):
        block = values[pl.ds(pl.multiple_of(o * TILE, TILE), TILE), :]
        block = jnp.where(level < NV, block, 1.0)
        choice = jnp.broadcast_to(mark_groups[pl.ds(o, 1), :], (TILE, LANES))
        parts = [jnp.where(choice == g, block, jnp.inf) for g in range(16)]
        start = pl.multiple_of(o * LANES, LANES)
        turned[pl.ds(start, LANES), :] = jnp.concatenate(parts, 0).T

    def spread_some(g, carry):
        for step in range(16):
            spread(g * 16 + step)
        return carry

    lax.fori_loop(0, owners // 16, spread_some, 0)
    spread(owners)

    loads[1].wait()
    loads[3].wait()

    def scatter(o, start, size):
        first = pl.multiple_of(o * LANES, LANES)
        for t in range(start, start + size):
            row = turned[pl.ds(first + t, 1), :]
            pltpu.store(rows.at[pl.ds(mark_rows[o, t], 1), :], row, mask=row < jnp.inf)

    def scatter_step(g, carry):
        for step in range(2):
            scatter(g * 2 + step, 0, 64)
        for step in range(2):
            for start, size in ((64, 64),):

                @pl.when(counts[g * 2 + step] > start)
                def _():
                    scatter(g * 2 + step, start, size)

        return carry

    lax.fori_loop(0, owners // 2, scatter_step, 0)
    scatter(owners, 0, LANES)

    def back(q):
        start = pl.multiple_of(q * LANES, LANES)
        turned[pl.ds(start, LANES), :] = rows[pl.ds(start, LANES), :].T

    def back_some(g, carry):
        for step in range(4):
            back(g * 4 + step)
        return carry

    lax.fori_loop(0, FILL_ROWS // LANES // 4, back_some, 0)

    for load in loads[4:]:
        load.wait()

    for c in range(NV):
        filled[c, 0:TILE, :] = jnp.zeros((TILE, LANES), jnp.float32)
        for plane, data in (
            (0, behind[c]),
            (1, field[c, 0:ROWS, :]),
            (CELL_PLANES, field[c, size - ROWS : size, :]),
            (CELL_PLANES + 1, ahead[c]),
        ):
            filled[c, TILE + plane * ROWS : TILE + (plane + 1) * ROWS, :] = data
    for edge in (0, size - ROWS):
        fringes[edge : edge + ROWS, :] = jnp.zeros((ROWS, LANES), jnp.float32)

    def merge(tile, carry):
        base = pl.multiple_of(tile * TILE, TILE)
        inner = pl.multiple_of(base + ROWS, TILE)
        flag = turned[pl.ds(base * TILE + NV, TILE, stride=TILE), :]
        fringes[pl.ds(inner, TILE), :] = flag
        for c in range(NV):
            filled[c, pl.ds(pl.multiple_of(inner + ROWS + TILE, TILE), TILE), :] = jnp.where(
                flag > 0.5,
                turned[pl.ds(base * TILE + c, TILE, stride=TILE), :],
                field[c, pl.ds(inner, TILE), :],
            )
        return carry

    lax.fori_loop(0, (CELL_PLANES - 2) * ROWS // TILE, merge, 0)

    def relax(i, carry):
        for part in range(ROWS // TILE):
            base = pl.multiple_of(i * ROWS + part * TILE, TILE)
            here = base + ROWS + TILE
            rate = ratio[pl.ds(base, TILE), :]
            scale = 1.0 / (1.0 + 6.0 * rate)
            fringe = fringes[pl.ds(base, TILE), :] > 0.5
            for c in range(NV):
                mid = filled[c, pl.ds(pl.multiple_of(here, TILE), TILE), :]
                up = filled[c, pl.ds(here + 1, TILE), :]
                down = filled[c, pl.ds(here - 1, TILE), :]
                if part == 0:
                    down = jnp.where(level == 0, 0.0, down)
                if part == ROWS // TILE - 1:
                    up = jnp.where(level == TILE - 1, 0.0, up)
                left = jnp.where(lane == 0, 0.0, pltpu.roll(mid, 1, 1))
                right = jnp.where(lane == LANES - 1, 0.0, pltpu.roll(mid, LANES - 1, 1))
                total = (
                    filled[c, pl.ds(pl.multiple_of(here + ROWS, TILE), TILE), :]
                    + filled[c, pl.ds(pl.multiple_of(here - ROWS, TILE), TILE), :]
                    + up
                    + down
                    + left
                    + right
                )
                result[c, pl.ds(base, TILE), :] = jnp.where(
                    fringe, mid, (mid + rate * total) * scale
                )
        plane_out(i).start()
        return carry

    def plane_out(i):
        plane = pl.ds(pl.multiple_of(i * ROWS, ROWS), ROWS)
        return pltpu.make_async_copy(result.at[:, plane], out.at[:, plane], out_sem.at[i])

    lax.fori_loop(0, CELL_PLANES, relax, 0)
    for i in range(CELL_PLANES):
        plane_out(i).wait()


def fill_and_relax(counts, mark_rows, mark_groups, values, field, behind, ahead, ratio):
    owners = counts.shape[1]
    size = CELL_PLANES * ROWS
    hbm = pl.BlockSpec(memory_space=pltpu.HBM)
    f32 = jnp.float32
    return pl.pallas_call(
        fill_kernel,
        out_shape=jax.ShapeDtypeStruct(field.shape, f32),
        in_specs=[hbm] * 8,
        out_specs=hbm,
        scratch_shapes=[
            pltpu.SMEM((owners,), jnp.int32),
            pltpu.SMEM(mark_rows.shape, jnp.int32),
            pltpu.VMEM(mark_groups.shape, jnp.int32),
            pltpu.VMEM(values.shape, f32),
            pltpu.VMEM(field.shape, f32),
            pltpu.VMEM(behind.shape, f32),
            pltpu.VMEM(ahead.shape, f32),
            pltpu.VMEM(ratio.shape, f32),
            pltpu.VMEM((max((owners + 1) * LANES, FILL_ROWS), LANES), f32),
            pltpu.VMEM((FILL_ROWS + TILE, LANES), f32),
            pltpu.VMEM((NV, size + 2 * ROWS + 2 * TILE, LANES), f32),
            pltpu.VMEM((size, LANES), f32),
            pltpu.VMEM(field.shape, f32),
            pltpu.SemaphoreType.DMA((8,)),
            pltpu.SemaphoreType.DMA((CELL_PLANES,)),
        ],
        compiler_params=pltpu.CompilerParams(vmem_limit_bytes=62 << 20),
        name="fill",
    )(counts, mark_rows, mark_groups, values, field, behind, ahead, ratio)


def on_device(
    field, node_jitter, time_ratio, donor_cell, receptor_offset, receptor_node, point_count
):
    flat_field = field.reshape(NV, CELL_PLANES * ROWS, LANES)
    answers, ahead, behind, mark_rows, mark_groups = donor_values(
        donor_cell[0],
        jnp.moveaxis(receptor_offset[0], 2, 1),
        flat_field,
        node_jitter.reshape(3, CELL_PLANES * ROWS, LANES),
        receptor_node[0],
        point_count,
    )
    out = fill_and_relax(
        point_count,
        mark_rows,
        mark_groups,
        answers,
        flat_field,
        behind,
        ahead,
        time_ratio.reshape(CELL_PLANES * ROWS, LANES),
    )
    return out.reshape(field.shape)


def solution(mesh):
    placed = (
        P(None, ("grid", "sub"), None, None),
        P(None, ("grid", "sub"), None, None),
        P(("grid", "sub"), None, None),
        P(("grid", "sub"), None, None, None),
        P(("grid", "sub"), None, None, None, None),
        P(("grid", "sub"), None, None, None),
        P(("grid", "sub"), None),
    )
    return jax.shard_map(
        on_device,
        mesh=mesh,
        in_specs=placed,
        out_specs=P(None, ("grid", "sub"), None, None),
        check_vma=False,
    )
```

```python
import jax
import jax.numpy as jnp
from jax import lax
from jax.experimental import pallas as pl
from jax.experimental.pallas import tpu as pltpu
from jax.sharding import PartitionSpec as P

LANES = 128
TILE = 8
ROWS = 32
CELL_PLANES = 8
PLANE = ROWS * LANES
NV = 5
UNROLL = 64
HALF_CELLS = CELL_PLANES // 2 * PLANE
FILL_ROWS = (CELL_PLANES - 2) * PLANE // 16


def lerp(low, high, weight):
    return low + weight * (high - low)


def solve_group(places, target):
    size = target[0].shape
    param = [jnp.full(size, 0.5, jnp.float32) for _ in range(3)]
    rise = [
        [[places[m][a][b][1] - places[m][a][b][0] for b in range(2)] for a in range(2)]
        for m in range(3)
    ]
    for _ in range(4):
        u, v, w = param
        misfit, jac = [], []
        for m in range(3):
            edge = [[places[m][a][b][0] + w * rise[m][a][b] for b in range(2)] for a in range(2)]
            across = [edge[a][1] - edge[a][0] for a in range(2)]
            face = [edge[a][0] + v * across[a] for a in range(2)]
            slope0 = face[1] - face[0]
            misfit.append(face[0] + u * slope0 - target[m])
            slope1 = lerp(across[0], across[1], u)
            slope2 = lerp(
                lerp(rise[m][0][0], rise[m][0][1], v), lerp(rise[m][1][0], rise[m][1][1], v), u
            )
            jac.append((slope0, slope1, slope2))
        x, y, z = ([jac[m][d] for m in range(3)] for d in range(3))

        def cross(p, q):
            return [
                p[1] * q[2] - p[2] * q[1],
                p[2] * q[0] - p[0] * q[2],
                p[0] * q[1] - p[1] * q[0],
            ]

        def dot(p, q):
            return p[0] * q[0] + p[1] * q[1] + p[2] * q[2]

        yz, zx, xy = cross(y, z), cross(z, x), cross(x, y)
        inverse = 1.0 / dot(x, yz)
        param = [
            u - dot(misfit, yz) * inverse,
            v - dot(misfit, zx) * inverse,
            w - dot(misfit, xy) * inverse,
        ]
    return param


def wrap(index, count):
    return index & (count - 1) if count & (count - 1) == 0 else lax.rem(index, count)


def donor_kernel(
    cells_hbm, offsets_hbm, field, jitter, nodes, counts,
    answers, ahead_out, behind_out, mark_rows_out, mark_groups_out,
    cells, offsets, ahead, behind, mark_rows, mark_groups, counts_now, cells_in, cells_near, cells_now, offsets_in, field_here, jitter_here, tiles, shifted, table, picked, corners, sent,
    local_sems, halo_send, halo_recv, cell_send, cell_recv, offset_send, offset_recv,
    answer_send, answer_recv,
):
    grids = lax.axis_size("grid")
    subs = lax.axis_size("sub")
    me = lax.axis_index("grid")
    sub = lax.axis_index("sub")
    after, before = wrap(me + 1, grids), wrap(me + grids - 1, grids)
    sub_after, sub_before = wrap(sub + 1, subs), wrap(sub + subs - 1, subs)

    barrier = pltpu.get_barrier_semaphore()

    def greet(s, carry):
        pl.semaphore_signal(barrier, inc=1, device_id={"grid": wrap(me + s, grids)})
        return carry

    lax.fori_loop(1, grids, greet, 0, unroll=7)
    pl.semaphore_signal(barrier, inc=1, device_id={"sub": sub_after})
    pl.semaphore_signal(barrier, inc=1, device_id={"sub": sub_before})

    loads = [
        pltpu.make_async_copy(field, field_here, local_sems.at[0]),
        pltpu.make_async_copy(jitter, jitter_here, local_sems.at[1]),
        pltpu.make_async_copy(cells_hbm, cells, local_sems.at[5]),
        pltpu.make_async_copy(offsets_hbm, offsets, local_sems.at[6]),
    ]
    side_loads = [
        pltpu.make_async_copy(counts.at[0], counts_now, local_sems.at[2]),
        pltpu.make_async_copy(nodes.at[:, 0], mark_rows.at[pl.ds(0, grids)], local_sems.at[3]),
        pltpu.make_async_copy(nodes.at[after, 1], mark_rows.at[grids], local_sems.at[4]),
    ]
    for load in loads + side_loads:
        load.start()
    for load in loads:
        load.wait()

    def put(start, data):
        tiles[pl.ds(start, TILE, stride=TILE), :] = data
        shifted[pl.ds(start, TILE, stride=TILE), :] = pltpu.roll(data, LANES - 1, 1)

    def fill(tile, carry):
        base = pl.multiple_of(tile * TILE, TILE)
        for c in range(NV):
            put(base * TILE + c, field_here[c, pl.ds(base, TILE), :])
        for c in range(3):
            put(base * TILE + NV + c, jitter_here[c, pl.ds(base, TILE), :])
        return carry

    lax.fori_loop(0, CELL_PLANES * ROWS // TILE, fill, 0)
    pl.semaphore_wait(barrier, grids + 1)

    def remote(source, target, send, recv, device):
        return pltpu.make_async_remote_copy(
            src_ref=source, dst_ref=target, send_sem=send, recv_sem=recv, device_id=device
        )

    first, last = pl.ds(0, ROWS), pl.ds((CELL_PLANES - 1) * ROWS, ROWS)
    halos = [
        remote(
            field_here.at[:, first], ahead.at[pl.ds(0, NV)],
            halo_send.at[0], halo_recv.at[0], {"sub": sub_before},
        ),
        remote(
            jitter_here.at[:, first], ahead.at[pl.ds(NV, 3)],
            halo_send.at[1], halo_recv.at[1], {"sub": sub_before},
        ),
        remote(
            field_here.at[:, last], behind, halo_send.at[2], halo_recv.at[2], {"sub": sub_after}
        ),
    ]
    for halo in halos:
        halo.start()

    def cell_copy(peer):
        return remote(
            cells.at[peer, 0], cells_in.at[me], cell_send.at[0], cell_recv.at[0], {"grid": peer}
        )

    def offset_copy(peer):
        return remote(
            offsets.at[peer, :, 0], offsets_in.at[pl.ds(me * TILE, 3)],
            offset_send.at[0], offset_recv.at[0], {"grid": peer},
        )

    def send_cells(s, carry):
        cell_copy(wrap(me + s, grids)).start()
        return carry

    def send_offsets(s, carry):
        offset_copy(wrap(me + s, grids)).start()
        return carry

    lax.fori_loop(1, grids, send_cells, 0, unroll=7)
    more_cells = remote(
        cells.at[after, 1], cells_in.at[grids], cell_send.at[1], cell_recv.at[1], {"grid": after}
    )
    more_cells.start()
    own_cells = pltpu.make_async_copy(cells.at[me, 0], cells_in.at[me], local_sems.at[0])
    own_cells.start()
    lax.fori_loop(1, grids, send_offsets, 0, unroll=7)
    more_offsets = remote(
        offsets.at[after, :, 1], offsets_in.at[pl.ds(grids * TILE, 3)],
        offset_send.at[1], offset_recv.at[1], {"grid": after},
    )
    more_offsets.start()
    own_offsets = pltpu.make_async_copy(
        offsets.at[me, :, 0], offsets_in.at[pl.ds(me * TILE, 3)], local_sems.at[1]
    )
    own_offsets.start()

    for load in side_loads:
        load.wait()
    slot = lax.broadcasted_iota(jnp.int32, (1, LANES), 1)

    def mark(o, live):
        node = mark_rows[pl.ds(o, 1), :]
        place = (((node >> 11) - 2) << 7) + (node & (LANES - 1))
        mark_rows[pl.ds(o, 1), :] = jnp.where(slot < live, place, FILL_ROWS)
        mark_groups[pl.ds(o, 1), :] = (node >> 7) & 15

    def mark_step(o, carry):
        mark(o, counts_now[o])
        return carry

    lax.fori_loop(0, grids, mark_step, 0)
    mark(grids, counts_now[after] - LANES)
    stores = [
        pltpu.make_async_copy(mark_rows, mark_rows_out, local_sems.at[3]),
        pltpu.make_async_copy(mark_groups, mark_groups_out, local_sems.at[4]),
        pltpu.make_async_copy(ahead, ahead_out, local_sems.at[5]),
        pltpu.make_async_copy(behind, behind_out, local_sems.at[6]),
    ]
    stores[0].start()
    stores[1].start()

    def build_some(q, carry):
        for step in range(4):
            row = q * 4 + step
            parts = []
            for half in range(2):
                for a in (0, 1, ROWS, ROWS + 1):
                    start = (row + half * (CELL_PLANES // 2) * ROWS + a) * TILE
                    start = pl.multiple_of(start, TILE)
                    parts.append(tiles[pl.ds(start, TILE), :])
                    parts.append(shifted[pl.ds(start, TILE), :])
            table[pl.ds(pl.multiple_of(row * LANES, LANES), LANES), :] = jnp.concatenate(
                parts, 0
            ).T
        return carry

    quarter = ROWS // 4
    lax.fori_loop(0, 3 * quarter, build_some, 0)
    for halo in halos:
        halo.wait_recv()
    stores[2].start()
    stores[3].start()
    for tile in range(ROWS // TILE):
        for c in range(8):
            put(
                (CELL_PLANES * ROWS + tile * TILE) * TILE + c,
                ahead[c, pl.ds(tile * TILE, TILE), :],
            )

    def drain(buffer, sem):
        pltpu.make_async_copy(buffer, buffer, sem).wait()

    drain(cells_in.at[pl.ds(0, grids - 1)], cell_recv.at[0])
    own_cells.wait()
    more_cells.wait_recv()
    cells_near[...] = cells_in[...] & (HALF_CELLS - 1)
    load_cells = pltpu.make_async_copy(cells_near, cells_now, local_sems.at[0])
    load_cells.start()
    lax.fori_loop(3 * quarter, 4 * quarter, build_some, 0)
    load_cells.wait()

    def pick(block, count):
        def one(r, carry):
            to = pl.multiple_of(r * LANES, LANES)
            for t in range(LANES):
                picked[pl.ds(to + t, 1), :] = table[pl.ds(cells_now[block + r, t], 1), :]
            return carry

        lax.fori_loop(0, count, one, 0, unroll=min(count, 2))

    def turn(block, r):
        values = picked[r * LANES : (r + 1) * LANES, :].T
        far = cells_in[pl.ds(block + r, 1), :] >= HALF_CELLS
        for q in range(8):
            corners[q, r * TILE : (r + 1) * TILE, :] = jnp.where(
                far, values[64 + 8 * q : 72 + 8 * q], values[8 * q : 8 * q + 8]
            )

    def solve(block):
        target = [
            offsets_in[pl.ds(block * TILE + m, TILE, stride=TILE), :] for m in range(3)
        ]
        places = [
            [
                [
                    [
                        corners[4 * a + 2 * b + d, pl.ds(NV + m, TILE, stride=TILE), :]
                        + float((a, b, d)[m])
                        for d in range(2)
                    ]
                    for b in range(2)
                ]
                for a in range(2)
            ]
            for m in range(3)
        ]
        u, v, w = solve_group(places, target)
        for c in range(NV):
            node = [corners[q, pl.ds(c, TILE, stride=TILE), :] for q in range(8)]
            edge = [lerp(node[2 * e], node[2 * e + 1], w) for e in range(4)]
            value = lerp(lerp(edge[0], edge[1], v), lerp(edge[2], edge[3], v), u)
            sent[pl.ds(block * TILE + c, TILE, stride=TILE), :] = value

    own_answer = pltpu.make_async_copy(
        sent.at[pl.ds(me * TILE, NV)], answers.at[pl.ds(me * TILE, NV)], local_sems.at[0]
    )

    def group(g, carry):
        block = pl.multiple_of(wrap((me >> 3) + g, grids // TILE) * TILE, TILE)
        pick(block, TILE)
        for r in range(TILE):
            turn(block, r)
        @pl.when(g == 0)
        def _():
            drain(picked.at[pl.ds(0, 3 * (grids - 1))], offset_recv.at[0])
            own_offsets.wait()
            more_offsets.wait_recv()

        solve(block)

        for r in range(TILE):
            peer = block + r

            @pl.when(peer != me)
            def _():
                remote(
                    sent.at[pl.ds(peer * TILE, NV)], answers.at[pl.ds(me * TILE, NV)],
                    answer_send.at[0], answer_recv.at[0], {"grid": peer},
                ).start()

            @pl.when(peer == me)
            def _():
                own_answer.start()

        return carry

    lax.fori_loop(0, grids // TILE, group, 0)
    pick(grids, 1)
    turn(grids, 0)
    solve(grids)
    more_answers = remote(
        sent.at[pl.ds(grids * TILE, NV)], answers.at[pl.ds(grids * TILE, NV)],
        answer_send.at[1], answer_recv.at[1], {"grid": before},
    )
    more_answers.start()

    drain(picked.at[pl.ds(0, NV * (grids - 1))], answer_recv.at[0])
    own_answer.wait()
    more_answers.wait()
    drain(picked.at[pl.ds(0, NV * (grids - 1))], answer_send.at[0])
    drain(cells_in.at[pl.ds(0, grids - 1)], cell_send.at[0])
    drain(picked.at[pl.ds(0, 3 * (grids - 1))], offset_send.at[0])
    more_cells.wait_send()
    more_offsets.wait_send()
    for halo in halos:
        halo.wait_send()
    for store in stores:
        store.wait()


def donor_values(cells, offsets, field, jitter, nodes, counts):
    grids = cells.shape[0]
    padded = grids + TILE
    node_rows = (CELL_PLANES + 1) * ROWS
    hbm = pl.BlockSpec(memory_space=pltpu.HBM)
    f32 = jnp.float32
    return pl.pallas_call(
        donor_kernel,
        out_shape=(
            jax.ShapeDtypeStruct(((grids + 1) * TILE, LANES), f32),
            jax.ShapeDtypeStruct((8, ROWS, LANES), f32),
            jax.ShapeDtypeStruct((NV, ROWS, LANES), f32),
            jax.ShapeDtypeStruct((padded, LANES), jnp.int32),
            jax.ShapeDtypeStruct((padded, LANES), jnp.int32),
        ),
        in_specs=[hbm] * 6,
        out_specs=(hbm,) * 5,
        scratch_shapes=[
            pltpu.VMEM(cells.shape, jnp.int32),
            pltpu.VMEM(offsets.shape, f32),
            pltpu.VMEM((8, ROWS, LANES), f32),
            pltpu.VMEM((NV, ROWS, LANES), f32),
            pltpu.VMEM((padded, LANES), jnp.int32),
            pltpu.VMEM((padded, LANES), jnp.int32),
            pltpu.SMEM((grids,), jnp.int32),
            pltpu.VMEM((padded, LANES), jnp.int32),
            pltpu.VMEM((padded, LANES), jnp.int32),
            pltpu.SMEM((padded, LANES), jnp.int32),
            pltpu.VMEM((padded * TILE, LANES), f32),
            pltpu.VMEM(field.shape, f32),
            pltpu.VMEM(jitter.shape, f32),
            pltpu.VMEM((node_rows * TILE + 2 * TILE, LANES), f32),
            pltpu.VMEM((node_rows * TILE + 2 * TILE, LANES), f32),
            pltpu.VMEM((HALF_CELLS, LANES), f32),
            pltpu.VMEM((TILE * LANES, LANES), f32),
            pltpu.VMEM((8, TILE * TILE, LANES), f32),
            pltpu.VMEM((padded * TILE, LANES), f32),
        ]
        + [pltpu.SemaphoreType.DMA((n,)) for n in (7, 3, 3, 2, 2, 2, 2, 2, 2)],
        compiler_params=pltpu.CompilerParams(
            collective_id=0, has_side_effects=True, vmem_limit_bytes=60 << 20
        ),
        name="donor",
    )(cells, offsets, field, jitter, nodes, counts)


def fill_kernel(
    counts_in, mark_rows_in, mark_groups_in, values_in, field_in, behind_in, ahead_in, ratio_in, out,
    counts, mark_rows, mark_groups, values, field, behind, ahead, ratio,
    turned, rows, filled, fringes, result, sems, out_sem,
):
    owners = counts.shape[0]
    loads = [
        pltpu.make_async_copy(source, target, sems.at[n])
        for n, (source, target) in enumerate(
            (
                (values_in, values),
                (mark_rows_in, mark_rows),
                (mark_groups_in, mark_groups),
                (counts_in.at[0], counts),
                (field_in, field),
                (behind_in, behind),
                (ahead_in, ahead),
                (ratio_in, ratio),
            )
        )
    ]
    for load in loads:
        load.start()
    size = CELL_PLANES * ROWS
    lane = lax.broadcasted_iota(jnp.int32, (TILE, LANES), 1)
    level = lax.broadcasted_iota(jnp.int32, (TILE, LANES), 0)

    def clear(q, carry):
        rows[pl.ds(pl.multiple_of(q * LANES, LANES), LANES), :] = jnp.zeros(
            (LANES, LANES), jnp.float32
        )
        return carry

    lax.fori_loop(0, FILL_ROWS // LANES, clear, 0)
    loads[0].wait()
    loads[2].wait()

    def spread(o):
        block = values[pl.ds(pl.multiple_of(o * TILE, TILE), TILE), :]
        block = jnp.where(level < NV, block, 1.0)
        choice = jnp.broadcast_to(mark_groups[pl.ds(o, 1), :], (TILE, LANES))
        parts = [jnp.where(choice == g, block, jnp.inf) for g in range(16)]
        start = pl.multiple_of(o * LANES, LANES)
        turned[pl.ds(start, LANES), :] = jnp.concatenate(parts, 0).T

    def spread_some(g, carry):
        for step in range(32):
            spread(g * 32 + step)
        return carry

    lax.fori_loop(0, owners // 32, spread_some, 0)
    spread(owners)

    loads[1].wait()
    loads[3].wait()

    def scatter(o, start, size):
        first = pl.multiple_of(o * LANES, LANES)
        for t in range(start, start + size):
            row = turned[pl.ds(first + t, 1), :]
            pltpu.store(rows.at[pl.ds(mark_rows[o, t], 1), :], row, mask=row < jnp.inf)

    def scatter_step(g, carry):
        for step in range(2):
            scatter(g * 2 + step, 0, 64)
        for step in range(2):
            for start, size in ((64, 64),):

                @pl.when(counts[g * 2 + step] > start)
                def _():
                    scatter(g * 2 + step, start, size)

        return carry

    lax.fori_loop(0, owners // 2, scatter_step, 0)
    scatter(owners, 0, LANES)

    def back(q):
        start = pl.multiple_of(q * LANES, LANES)
        turned[pl.ds(start, LANES), :] = rows[pl.ds(start, LANES), :].T

    def back_some(g, carry):
        for step in range(12):
            back(g * 12 + step)
        return carry

    lax.fori_loop(0, FILL_ROWS // LANES // 12, back_some, 0)

    for load in loads[4:]:
        load.wait()

    for c in range(NV):
        filled[c, 0:TILE, :] = jnp.zeros((TILE, LANES), jnp.float32)
        for plane, data in (
            (0, behind[c]),
            (1, field[c, 0:ROWS, :]),
            (CELL_PLANES, field[c, size - ROWS : size, :]),
            (CELL_PLANES + 1, ahead[c]),
        ):
            filled[c, TILE + plane * ROWS : TILE + (plane + 1) * ROWS, :] = data
    for edge in (0, size - ROWS):
        fringes[edge : edge + ROWS, :] = jnp.zeros((ROWS, LANES), jnp.float32)

    def merge(tile, carry):
        base = pl.multiple_of(tile * TILE, TILE)
        inner = pl.multiple_of(base + ROWS, TILE)
        flag = turned[pl.ds(base * TILE + NV, TILE, stride=TILE), :]
        fringes[pl.ds(inner, TILE), :] = flag
        for c in range(NV):
            filled[c, pl.ds(pl.multiple_of(inner + ROWS + TILE, TILE), TILE), :] = jnp.where(
                flag > 0.5,
                turned[pl.ds(base * TILE + c, TILE, stride=TILE), :],
                field[c, pl.ds(inner, TILE), :],
            )
        return carry

    lax.fori_loop(0, (CELL_PLANES - 2) * ROWS // TILE, merge, 0, unroll=2)

    def relax(i, carry):
        for part in range(ROWS // TILE):
            base = pl.multiple_of(i * ROWS + part * TILE, TILE)
            here = base + ROWS + TILE
            rate = ratio[pl.ds(base, TILE), :]
            scale = 1.0 / (1.0 + 6.0 * rate)
            fringe = fringes[pl.ds(base, TILE), :] > 0.5
            for c in range(NV):
                mid = filled[c, pl.ds(pl.multiple_of(here, TILE), TILE), :]
                up = filled[c, pl.ds(here + 1, TILE), :]
                down = filled[c, pl.ds(here - 1, TILE), :]
                if part == 0:
                    down = jnp.where(level == 0, 0.0, down)
                if part == ROWS // TILE - 1:
                    up = jnp.where(level == TILE - 1, 0.0, up)
                left = jnp.where(lane == 0, 0.0, pltpu.roll(mid, 1, 1))
                right = jnp.where(lane == LANES - 1, 0.0, pltpu.roll(mid, LANES - 1, 1))
                total = (
                    filled[c, pl.ds(pl.multiple_of(here + ROWS, TILE), TILE), :]
                    + filled[c, pl.ds(pl.multiple_of(here - ROWS, TILE), TILE), :]
                    + up
                    + down
                    + left
                    + right
                )
                result[c, pl.ds(base, TILE), :] = jnp.where(
                    fringe, mid, (mid + rate * total) * scale
                )
        plane_out(i).start()
        return carry

    def plane_out(i):
        plane = pl.ds(pl.multiple_of(i * ROWS, ROWS), ROWS)
        return pltpu.make_async_copy(result.at[:, plane], out.at[:, plane], out_sem.at[i])

    lax.fori_loop(0, CELL_PLANES, relax, 0)
    for i in range(CELL_PLANES):
        plane_out(i).wait()


def fill_and_relax(counts, mark_rows, mark_groups, values, field, behind, ahead, ratio):
    owners = counts.shape[1]
    size = CELL_PLANES * ROWS
    hbm = pl.BlockSpec(memory_space=pltpu.HBM)
    f32 = jnp.float32
    return pl.pallas_call(
        fill_kernel,
        out_shape=jax.ShapeDtypeStruct(field.shape, f32),
        in_specs=[hbm] * 8,
        out_specs=hbm,
        scratch_shapes=[
            pltpu.SMEM((owners,), jnp.int32),
            pltpu.SMEM(mark_rows.shape, jnp.int32),
            pltpu.VMEM(mark_groups.shape, jnp.int32),
            pltpu.VMEM(values.shape, f32),
            pltpu.VMEM(field.shape, f32),
            pltpu.VMEM(behind.shape, f32),
            pltpu.VMEM(ahead.shape, f32),
            pltpu.VMEM(ratio.shape, f32),
            pltpu.VMEM((max((owners + 1) * LANES, FILL_ROWS), LANES), f32),
            pltpu.VMEM((FILL_ROWS + TILE, LANES), f32),
            pltpu.VMEM((NV, size + 2 * ROWS + 2 * TILE, LANES), f32),
            pltpu.VMEM((size, LANES), f32),
            pltpu.VMEM(field.shape, f32),
            pltpu.SemaphoreType.DMA((8,)),
            pltpu.SemaphoreType.DMA((CELL_PLANES,)),
        ],
        compiler_params=pltpu.CompilerParams(vmem_limit_bytes=62 << 20),
        name="fill",
    )(counts, mark_rows, mark_groups, values, field, behind, ahead, ratio)


def on_device(
    field, node_jitter, time_ratio, donor_cell, receptor_offset, receptor_node, point_count
):
    flat_field = field.reshape(NV, CELL_PLANES * ROWS, LANES)
    answers, ahead, behind, mark_rows, mark_groups = donor_values(
        donor_cell[0],
        jnp.moveaxis(receptor_offset[0], 2, 1),
        flat_field,
        node_jitter.reshape(3, CELL_PLANES * ROWS, LANES),
        receptor_node[0],
        point_count,
    )
    out = fill_and_relax(
        point_count,
        mark_rows,
        mark_groups,
        answers,
        flat_field,
        behind,
        ahead,
        time_ratio.reshape(CELL_PLANES * ROWS, LANES),
    )
    return out.reshape(field.shape)


def solution(mesh):
    placed = (
        P(None, ("grid", "sub"), None, None),
        P(None, ("grid", "sub"), None, None),
        P(("grid", "sub"), None, None),
        P(("grid", "sub"), None, None, None),
        P(("grid", "sub"), None, None, None, None),
        P(("grid", "sub"), None, None, None),
        P(("grid", "sub"), None),
    )
    return jax.shard_map(
        on_device,
        mesh=mesh,
        in_specs=placed,
        out_specs=P(None, ("grid", "sub"), None, None),
        check_vma=False,
    )
```
